512 devices in a mesh: gy: 16 (over z, core), gx: 32 (over y, x).
Axes of the slice: x: 4, y: 8, z: 8, core: 2. Of those that a mesh axis runs over, the one named last changes fastest.
Arguments:
- atm_flux: bfloat16 [16, 64, 2, 128], P('gy', 'gx'), may hold values from -6 to 6
- remap_source: int32 [256, 32, 2], P('gy', 'gx'), may hold values from 0 to 5
- remap_weight: bfloat16 [256, 32, 2, 128, 128], P('gy', 'gx'), may hold values from -0.375 to 0.375
- tracers: float32 [2, 62, 256, 4096], P(None, None, 'gy', 'gx'), may hold values from -6 to 6
- velocity: float32 [2, 62, 256, 4096], P(None, None, 'gy', 'gx'), may hold values from -1.5 to 1.5
- vert_diff: float32 [61, 256, 4096], P(None, 'gy', 'gx'), may hold values from 0.05 to 5
- ocean_depth: float32 [256, 4096], P('gy', 'gx'), may hold values from 0.25 to 1
- surface_term: float32 [256, 4096], P('gy', 'gx'), may hold values from 0.05 to 0.5
- land_mask: int32 [64, 32], P('gy', 'gx'), may hold values from 0 to 1, as said below
- barotropic_block_map: int32 [16, 96], P('gy'), may hold values from -1 to 127, as said below
Outputs:
- new_tracers: float32 [2, 62, 256, 4096], P(None, None, 'gy', 'gx')
- sea_level: float32 [16, 96, 4, 128], P('gy', 'gx')
- barotropic_slot_residual: float32 [16, 96, 4, 128], P('gy', 'gx')
The draws below stay inside these ranges and needn't reach their ends.
Inputs may be any that keep to these rules, and one draw needn't show every extreme that they name: `land_mask`: 1 marks an ocean block, 0 a land block; some blocks of every device row are ocean. `barotropic_block_map`: entry d * 3 + s of device row i names the block held in slot s of device d of that row as (gx index of its home device) * 4 + (its block index on that device), or -1 for an empty slot; every ocean block of the row appears exactly once and no land block appears; the device holding a block is its home device or one of the two next to it along gx, periodically; some device holds 3 blocks.
All inputs are finite; a program needn't handle non-finite values.
Results may differ from the reference program's by a relative error of at most 0.0003.
Values may be sent and summed in bfloat16 or wider, within the bound.
A program may use at most 64 MiB of HBM per device.

```python
import math
import jax
import jax.numpy as jnp
from jax import lax

CY = 16
DEVICE_COLUMNS = 128
BLOCK_GRID_ROWS = 4
LV = 62
NTR = 2
AB = 2
ACELL = 128
K = 2
ITERS = 2
OB = 4
CAPB = 3
NY = 256
NX = 4096
NA = 64
BAROTROPIC_SLOTS = 96
N_GY = 16
N_GX = 32


def layout_draw(seed_key):
    sub_keys = jax.random.split(seed_key, 7)
    pair_count = N_GX // 2
    first_count = jax.random.randint(sub_keys[0], (N_GY, pair_count), 0, OB + 1)
    second_limit = jnp.minimum(OB, 2 * CAPB - first_count)
    second_count = jax.random.randint(sub_keys[1], (N_GY, pair_count), 0, second_limit + 1)
    flipped = jax.random.randint(sub_keys[2], (N_GY, pair_count), 0, 2)
    shift_rows = jax.random.randint(sub_keys[5], (N_GY, 1), 0, 2)
    row_column = jnp.arange(N_GY)[:, None]
    forced = row_column < 4
    first_count = jnp.where(forced, OB, first_count)
    second_count = jnp.where(forced, OB - 2, second_count)
    flipped = jnp.where(forced, row_column // 2 % 2, flipped)
    shift_rows = jnp.where(forced, row_column % 2, shift_rows)
    left_count = jnp.where(flipped == 1, second_count, first_count)
    right_count = jnp.where(flipped == 1, first_count, second_count)
    left_column = jnp.mod(2 * jnp.arange(pair_count)[None, :] + shift_rows, N_GX)
    right_column = jnp.mod(left_column + 1, N_GX)
    row_index = jnp.broadcast_to(jnp.arange(N_GY)[:, None], (N_GY, pair_count))
    ocean_count = jnp.zeros((N_GY, N_GX), jnp.int32)
    ocean_count = ocean_count.at[row_index, left_column].set(left_count).at[row_index, right_column].set(right_count)
    partner = jnp.zeros((N_GY, N_GX), jnp.int32)
    partner = partner.at[row_index, left_column].set(right_column).at[row_index, right_column].set(left_column)
    scores = jax.random.randint(sub_keys[6], (N_GY, N_GX, OB), 0, 1 << 20) * OB + jnp.arange(OB)[None, None, :]
    ocean_rank = jnp.argsort(jnp.argsort(scores, axis=-1, stable=True), axis=-1, stable=True)
    is_ocean = ocean_rank < ocean_count[:, :, None]
    land_mask = jnp.transpose(is_ocean.astype(jnp.int32), (0, 2, 1)).reshape(N_GY * OB, N_GX)
    ocean_order = jnp.cumsum(is_ocean.astype(jnp.int32), axis=-1) - 1
    column_grid = jnp.broadcast_to(jnp.arange(N_GX)[None, :, None], (N_GY, N_GX, OB))
    keep_home = ocean_order < CAPB
    dest_device = jnp.where(keep_home, column_grid, partner[:, :, None])
    partner_count = jnp.take_along_axis(ocean_count, partner, axis=1)[:, :, None]
    slot_index = jnp.where(keep_home, ocean_order, partner_count)
    target_slot = jnp.where(is_ocean, dest_device * CAPB + slot_index, N_GX * CAPB)
    block_code = column_grid * OB + jnp.arange(OB)[None, None, :]
    row_grid = jnp.broadcast_to(jnp.arange(N_GY)[:, None, None], (N_GY, N_GX, OB))
    barotropic_block_map = jnp.full((N_GY, N_GX * CAPB), -1, jnp.int32)
    barotropic_block_map = barotropic_block_map.at[row_grid, target_slot].set(block_code.astype(jnp.int32), mode='drop')
    return (land_mask.astype(jnp.int32), barotropic_block_map)


def draw_land_mask(key, part):
    return layout_draw(jax.random.fold_in(key, 11))[0]


def draw_barotropic_block_map(key, part):
    return layout_draw(jax.random.fold_in(key, 11))[1]


def place_ends(entries, key, low, largest):
    shape = entries.shape
    spot = [jax.random.randint(jax.random.fold_in(key, axis), (), 0, shape[axis]) for axis in range(len(shape))]
    entries = entries.at[tuple(spot)].set(low)
    longest = shape.index(max(shape))
    spot[longest] = (spot[longest] + 1) % shape[longest]
    return entries.at[tuple(spot)].set(largest)


def steps_of(own_key, extent, shards, smallest, top_value):
    loudness = 1.0
    for axis_at, shards_of in shards:
        steps = jax.random.uniform(jax.random.fold_in(jax.random.fold_in(own_key, 6), axis_at), (shards_of,), jnp.float32, smallest / len(shards), top_value / len(shards))
        loudness = loudness * jnp.repeat(jnp.exp(steps), extent[axis_at] // shards_of).reshape((-1,) + (1,) * (len(extent) - 1 - axis_at))
    return loudness


def noise(rng, extent, width, most, pieces=(), kind=jnp.bfloat16):
    gain = steps_of(rng, extent, pieces, -0.22, 0.18) if pieces else 1.0
    entries = jax.random.normal(rng, extent, jnp.float32) * width * gain
    return jnp.minimum(jnp.maximum(entries, -most), most).astype(kind)


def setup_inputs(seed: int = 0) -> dict:
    splits = jax.random.split(jax.random.key(seed), 11)
    atm_flux = noise(splits[0], (N_GY, NA, NTR, ACELL), 1.0, 6.0, ((0, 16), (1, 32)))
    remap_source = place_ends(jax.random.randint(splits[1], (NY, N_GX, K), 0, 3 * AB), jax.random.fold_in(splits[1], 1), 0, (3 * AB) - 1).astype(jnp.int32)
    remap_weight = noise(splits[2], (NY, N_GX, K, DEVICE_COLUMNS, ACELL), (K * ACELL) ** -0.5, 0.375, ((0, 16), (1, 32)))
    tracers = noise(splits[3], (NTR, LV, NY, NX), 1.0, 6.0, ((2, 16), (3, 32)), jnp.float32)
    velocity = noise(splits[4], (2, LV, NY, NX), 0.25, 1.5, ((2, 16), (3, 32)), jnp.float32)
    vert_diff = jnp.clip(jnp.exp(math.log(5.0) - 4.6051702 * jax.random.uniform(splits[5], (LV - 1, NY, NX), jnp.float32) ** steps_of(splits[5], (LV - 1, NY, NX), ((1, 16), (2, 32)), -0.2, 0.2)), 0.05, 5.0)
    ocean_depth = jnp.clip(jnp.exp(math.log(1.0) - 1.3862944 * jax.random.uniform(splits[6], (NY, NX), jnp.float32) ** steps_of(splits[6], (NY, NX), ((0, 16), (1, 32)), -0.2, 0.2)), 0.25, 1.0)
    surface_term = jnp.clip(jnp.exp(math.log(0.5) - 2.3025851 * jax.random.uniform(splits[7], (NY, NX), jnp.float32) ** steps_of(splits[7], (NY, NX), ((0, 16), (1, 32)), -0.2, 0.2)), 0.05, 0.5)
    land_mask = draw_land_mask(jax.random.fold_in(splits[10], 71), 0)
    barotropic_block_map = draw_barotropic_block_map(jax.random.fold_in(splits[10], 71), 0)
    return {"atm_flux": atm_flux, "remap_source": remap_source, "remap_weight": remap_weight, "tracers": tracers, "velocity": velocity, "vert_diff": vert_diff, "ocean_depth": ocean_depth, "surface_term": surface_term, "land_mask": land_mask, "barotropic_block_map": barotropic_block_map}


diffusivity = 0.1
flux_gain = 0.5

def upwind(flow_speed, behind, centre, forward, beyond, face_mask):
    centred = (7.0 * (centre + forward) - behind - beyond) / 12.0
    curved = (3.0 * (centre - forward) + beyond - behind) / 12.0
    return face_mask * (flow_speed * centred - jnp.abs(flow_speed) * curved - diffusivity * (forward - centre))

def implicit_mix(provisional, vert_diff):
    levels = provisional.shape[1]
    zero_plane = jnp.zeros_like(vert_diff[0])
    cprime = []
    dprime = []
    for level_index in range(levels):
        lower_coef = vert_diff[level_index - 1] if level_index > 0 else zero_plane
        upper_coef = vert_diff[level_index] if level_index < levels - 1 else zero_plane
        centre = 1.0 + lower_coef + upper_coef
        if level_index == 0:
            divisor = centre
            solved = provisional[:, 0] / divisor
        else:
            divisor = centre + lower_coef * cprime[-1]
            solved = (provisional[:, level_index] + lower_coef * dprime[-1]) / divisor
        cprime.append(-upper_coef / divisor)
        dprime.append(solved)
    result = [dprime[-1]]
    for level_index in range(levels - 2, -1, -1):
        result.append(dprime[level_index] - cprime[level_index] * result[-1])
    return jnp.stack(result[::-1], axis=1)

def reference(atm_flux, remap_source, remap_weight, tracers, velocity, vert_diff, ocean_depth, surface_term, land_mask, barotropic_block_map):
    cell_mask = jnp.repeat(jnp.repeat(land_mask.astype(jnp.float32), BLOCK_GRID_ROWS, axis=0), DEVICE_COLUMNS, axis=1)
    row_owner = (jnp.arange(NY) // CY).astype(jnp.int32)
    col_start = (jnp.arange(N_GX) * AB - AB).astype(jnp.int32)
    atm_column = jnp.mod(col_start[None, :, None] + remap_source, NA).astype(jnp.int32)
    picked = atm_flux[row_owner[:, None, None], atm_column]

    def remap_row(inputs):
        weight_row, picked_row = inputs
        return jnp.einsum('jkca,jkfa->fjc', weight_row.astype(jnp.float32), picked_row.astype(jnp.float32), precision=lax.Precision.HIGHEST)
    surface_flux = lax.map(remap_row, (remap_weight, picked))
    surface_flux = jnp.transpose(surface_flux, (1, 0, 2, 3)).reshape(NTR, NY, NX)
    mask_pad = jnp.pad(cell_mask, ((1, 1), (0, 0)))
    east_open = cell_mask * jnp.roll(cell_mask, -1, axis=1)
    north_open = mask_pad[:NY + 1] * mask_pad[1:NY + 2]

    def level_step(level_index):
        layer = lax.dynamic_index_in_dim(tracers, level_index, 1, keepdims=False) * cell_mask
        speeds = lax.dynamic_index_in_dim(velocity, level_index, 1, keepdims=False)
        east_flux = upwind(speeds[0], jnp.roll(layer, 1, axis=-1), layer, jnp.roll(layer, -1, axis=-1), jnp.roll(layer, -2, axis=-1), east_open)
        east_div = east_flux - jnp.roll(east_flux, 1, axis=-1)
        padded_layer = jnp.pad(layer, ((0, 0), (2, 2), (0, 0)))
        north_speed = jnp.pad(speeds[1], ((1, 0), (0, 0)))[:NY + 1]
        north_flux = upwind(north_speed, padded_layer[:, 0:NY + 1], padded_layer[:, 1:NY + 2], padded_layer[:, 2:NY + 3], padded_layer[:, 3:NY + 4], north_open)
        north_div = north_flux[:, 1:] - north_flux[:, :-1]
        return cell_mask * (layer - east_div - north_div)
    provisional = jnp.transpose(lax.map(level_step, jnp.arange(LV, dtype=jnp.int32)), (1, 0, 2, 3))
    provisional = provisional.at[:, 0].add(flux_gain * (cell_mask * surface_flux))
    new_tracers = implicit_mix(provisional, vert_diff)
    forcing = cell_mask * lax.optimization_barrier(jnp.sum(new_tracers[0] - new_tracers[1], axis=0)) * (1.0 / math.sqrt(2.0 * LV))
    zero_row = jnp.zeros((1, NX), jnp.float32)
    mask_next = jnp.concatenate([cell_mask[1:], zero_row], axis=0)
    depth_next = jnp.concatenate([ocean_depth[1:], zero_row], axis=0)
    east_weight = cell_mask * jnp.roll(cell_mask, -1, axis=1) * (ocean_depth + jnp.roll(ocean_depth, -1, axis=1)) * 0.5
    west_weight = jnp.roll(east_weight, 1, axis=1)
    north_weight = cell_mask * mask_next * (ocean_depth + depth_next) * 0.5
    south_weight = jnp.concatenate([zero_row, north_weight[:-1]], axis=0)
    diagonal = cell_mask * surface_term + (1.0 - cell_mask) + east_weight + west_weight + north_weight + south_weight
    inverse = 1.0 / diagonal

    def operate(field):
        east_value = jnp.roll(field, -1, axis=1)
        west_value = jnp.roll(field, 1, axis=1)
        north_value = jnp.concatenate([field[1:], zero_row], axis=0)
        south_value = jnp.concatenate([zero_row, field[:-1]], axis=0)
        return diagonal * field - east_weight * east_value - west_weight * west_value - north_weight * north_value - south_weight * south_value
    solution = jnp.zeros_like(forcing)
    residual = forcing
    precond = inverse * residual
    direction = precond
    rho_now = jnp.sum(residual * precond)
    for repeat in range(ITERS):
        image_field = operate(direction)
        step_size = rho_now / jnp.sum(direction * image_field)
        solution = solution + step_size * direction
        residual = residual - step_size * image_field
        if repeat + 1 < ITERS:
            precond = inverse * residual
            rho_next = jnp.sum(residual * precond)
            direction = precond + rho_next / rho_now * direction
            rho_now = rho_next

    def to_slots(field):
        blocks = field.reshape(N_GY, OB, BLOCK_GRID_ROWS, N_GX, DEVICE_COLUMNS).transpose(0, 3, 1, 2, 4).reshape(N_GY, N_GX * OB, BLOCK_GRID_ROWS, DEVICE_COLUMNS)
        grid_of_index = jnp.broadcast_to(jnp.maximum(barotropic_block_map, 0).astype(jnp.int32)[:, :, None, None], (N_GY, BAROTROPIC_SLOTS, BLOCK_GRID_ROWS, DEVICE_COLUMNS))
        chosen = jnp.take_along_axis(blocks, grid_of_index, axis=1)
        return jnp.where((barotropic_block_map >= 0)[:, :, None, None], chosen, 0.0)
    return (new_tracers, to_slots(solution), to_slots(residual))
```

```python
import functools
import math

import jax
import jax.numpy as jnp
from jax import lax
from jax.experimental import pallas as pl
from jax.experimental.pallas import tpu as pltpu
from jax.sharding import PartitionSpec as P

DIFFUSIVITY = 0.1
FLUX_GAIN = 0.5
MESH = pl.DeviceIdType.MESH
GROUP = 8
SIDES = ((0, 1), (0, -1), (1, 0), (-1, 0), (1, 1), (1, -1), (-1, 1), (-1, -1))
META, ATM, EDGE, SEARCH, SLOT, REDUCE = 0, 8, 10, 16, 24, 26
COPIES = REDUCE + 3 * (GROUP - 1)


def flux(speed, behind, centre, forward, beyond, mixing):
    drop = centre - forward
    return (
        speed * (7.0 * (centre + forward) - (behind + beyond))
        - jnp.abs(speed) * (3.0 * drop + (beyond - behind))
        + mixing * drop
    )


def kernel(
    n_gy,
    n_gx,
    source_ref,
    land_ref,
    map_ref,
    atm_ref,
    depth_ref,
    surface_ref,
    weight_hbm,
    tracer_hbm,
    velocity_hbm,
    vert_hbm,
    new_hbm,
    sea_ref,
    slot_ref,
    weight,
    cells,
    east_speed,
    north_speed,
    vert,
    meta_own,
    meta,
    atm_own,
    atm_near,
    to_north,
    to_south,
    from_south,
    from_north,
    speed_north,
    speed_south,
    edge_own,
    edge_near,
    speed_east,
    speed_west,
    west_face,
    surface_flux,
    factor,
    solved,
    search_own,
    search,
    fields,
    fields_near,
    partial,
    gathered,
    placed,
    local_sem,
    send_sem,
    recv_sem,
):
    tracer_count, levels, rows, cols = tracer_hbm.shape
    gy = lax.axis_index("gy")
    gx = lax.axis_index("gx")

    loads = [
        pltpu.make_async_copy(tracer_hbm, cells.at[:, :, 8 : 8 + rows, :], local_sem.at[0]),
        pltpu.make_async_copy(velocity_hbm.at[0], east_speed, local_sem.at[1]),
        pltpu.make_async_copy(
            velocity_hbm.at[1], north_speed.at[:, 8 : 8 + rows, :], local_sem.at[2]
        ),
        pltpu.make_async_copy(weight_hbm, weight, local_sem.at[3]),
        pltpu.make_async_copy(vert_hbm, vert.at[1:levels], local_sem.at[4]),
    ]
    for load in loads:
        load.start()

    def beside(dy, dx):
        return (lax.rem(gy + dy + n_gy, n_gy), lax.rem(gx + dx + n_gx, n_gx))

    inner_gy, inner_gx = n_gy // GROUP, n_gx // GROUP
    core, column = lax.rem(gy, inner_gy), lax.rem(gx, inner_gx)
    flat = core * inner_gx + column

    def partner(stage, k):
        if stage == 0:
            other = lax.rem(flat + k, GROUP)
            return (gy - core + other // inner_gx, gx - column + lax.rem(other, inner_gx))
        if stage == 1:
            return (gy, lax.rem(gx + k * inner_gx, n_gx))
        return (lax.rem(gy + k * inner_gy, n_gy), gx)

    barrier = pltpu.get_barrier_semaphore()
    peers = [beside(dy, dx) for dy, dx in SIDES]
    peers += [partner(stage, k) for stage in range(3) for k in range(1, GROUP)]
    for peer in peers:
        pl.semaphore_signal(barrier, inc=1, device_id=peer, device_id_type=MESH)

    def remote(index, src, dst, device):
        copy = pltpu.make_async_remote_copy(
            src_ref=src,
            dst_ref=dst,
            send_sem=send_sem.at[index],
            recv_sem=recv_sem.at[index],
            device_id=device,
            device_id_type=MESH,
        )
        copy.start()
        return copy

    def sides(first, own, padded):
        lead = (slice(None),) * (len(own.shape) - 2)
        source_rows = {0: slice(0, rows), 1: slice(rows - 8, rows), -1: slice(0, 8)}
        target_rows = {0: slice(8, 8 + rows), 1: slice(0, 8), -1: slice(8 + rows, 16 + rows)}
        target_cols = {
            0: slice(cols, 2 * cols),
            1: slice(0, cols),
            -1: slice(2 * cols, 3 * cols),
        }
        return [
            remote(
                first + k,
                own.at[lead + (source_rows[dy],)],
                padded.at[lead + (target_rows[dy], target_cols[dx])],
                beside(dy, dx),
            )
            for k, (dy, dx) in enumerate(SIDES)
        ]

    row = lax.broadcasted_iota(jnp.int32, (rows, cols), 0)
    lane = lax.broadcasted_iota(jnp.int32, (rows, cols), 1)
    block_rows = rows // land_ref.shape[0]
    mask = jnp.zeros((rows, cols), jnp.float32)
    for block in range(land_ref.shape[0]):
        wet = land_ref[block, 0].astype(jnp.float32)
        mask = jnp.where(row // block_rows == block, wet, mask)
    meta_own[0] = mask
    meta_own[1] = depth_ref[...]
    meta_own[2] = surface_ref[...]
    for k in range(3):
        meta[k, 8 : 8 + rows, cols : 2 * cols] = meta_own[k]
    atm_own[...] = atm_ref[0].astype(jnp.float32)
    blocks_near = atm_own.shape[0]
    atm_near[blocks_near : 2 * blocks_near] = atm_own[...]

    pl.semaphore_wait(barrier, len(peers))
    sent = sides(META, meta_own, meta)
    meta_copies = list(sent)
    atm_copies = [
        remote(ATM, atm_own, atm_near.at[0:blocks_near], beside(0, 1)),
        remote(ATM + 1, atm_own, atm_near.at[2 * blocks_near : 3 * blocks_near], beside(0, -1)),
    ]

    loads[0].wait()
    zero = jnp.zeros((rows, cols), jnp.float32)
    pair = lane // 2

    def pack(level, packed):
        packed = list(packed)
        here = pair == level
        for f in range(tracer_count):
            values = cells[f, level, 8 : 8 + rows, :] * mask
            cells[f, level, 8 : 8 + rows, :] = values
            to_north[f, level] = values[rows - 2 :]
            to_south[f, level] = values[:2]
            packed[2 * f] = jnp.where(here, pltpu.roll(values, 2 * level, 1), packed[2 * f])
            packed[2 * f + 1] = jnp.where(
                here, pltpu.roll(values, lax.rem(2 * level + 2, cols), 1), packed[2 * f + 1]
            )
        return tuple(packed)

    packed = lax.fori_loop(0, levels, pack, (zero,) * (2 * tracer_count), unroll=2)
    for f in range(tracer_count):
        edge_own[0, f] = packed[2 * f]
        edge_own[1, f] = packed[2 * f + 1]
    edge_copies = [
        remote(EDGE, to_north, from_south, beside(1, 0)),
        remote(EDGE + 1, to_south, from_north, beside(-1, 0)),
        remote(EDGE + 2, edge_own.at[0], edge_near.at[0], beside(0, -1)),
        remote(EDGE + 3, edge_own.at[1], edge_near.at[1], beside(0, 1)),
    ]

    loads[1].wait()
    loads[2].wait()

    def pack_speed(level, packed):
        speed_north[pl.ds(level, 1), :] = north_speed[level, 7 + rows : 8 + rows, :]
        return jnp.where(
            pair == level,
            pltpu.roll(east_speed[level], lax.rem(2 * level + 1, cols), 1),
            packed,
        )

    speed_east[...] = lax.fori_loop(0, levels, pack_speed, zero, unroll=2)
    edge_copies += [
        remote(EDGE + 4, speed_north, speed_south, beside(1, 0)),
        remote(EDGE + 5, speed_east, speed_west, beside(0, 1)),
    ]

    loads[3].wait()
    for copy in atm_copies:
        copy.wait_recv()

    def remap(r, carry):
        total = jnp.zeros((tracer_count, cols), jnp.float32)
        for k in range(weight.shape[2]):
            picked = atm_near[source_ref[r, 0, k]].astype(jnp.bfloat16)
            total += lax.dot_general(
                picked,
                weight[r, 0, k],
                (((1,), (1,)), ((), ())),
                preferred_element_type=jnp.float32,
            )
        for f in range(tracer_count):
            surface_flux[f, pl.ds(r, 1), :] = total[f : f + 1]
        return carry

    lax.fori_loop(0, rows, remap, 0, unroll=4)
    for f in range(tracer_count):
        surface_flux[f] = FLUX_GAIN * mask * surface_flux[f]

    for copy in meta_copies:
        copy.wait_recv()
    height, width = search.shape
    wide_row = lax.broadcasted_iota(jnp.int32, (height, width), 0)
    below = jnp.where(gy > 0, 1.0, 0.0)
    above = jnp.where(gy < n_gy - 1, 1.0, 0.0)
    inside = jnp.where(wide_row < 8, below, jnp.where(wide_row >= 8 + rows, above, 1.0))
    wide_mask = meta[0] * inside
    depth = meta[1]

    def next_col(v):
        return pltpu.roll(v, width - 1, 1)

    def last_col(v):
        return pltpu.roll(v, 1, 1)

    def next_row(v):
        return pltpu.roll(v, height - 1, 0)

    def last_row(v):
        return pltpu.roll(v, 1, 0)

    wide_east = wide_mask * next_col(wide_mask)
    wide_north = wide_mask * next_row(wide_mask)
    east_weight = wide_east * (depth + next_col(depth)) * 0.5
    north_weight = wide_north * (depth + next_row(depth)) * 0.5
    west_weight = last_col(east_weight)
    south_weight = last_row(north_weight)
    diagonal = (
        wide_mask * meta[2]
        + (1.0 - wide_mask)
        + east_weight
        + west_weight
        + north_weight
        + south_weight
    )
    inverse = 1.0 / diagonal
    wide_south = last_row(wide_north)
    wide_west = last_col(wide_east)

    def centre(v):
        return v[8 : 8 + rows, cols : 2 * cols]

    east_open = centre(wide_east) * (1.0 / 12.0)
    north_open = centre(wide_north) * (1.0 / 12.0)
    south_open = centre(wide_south) * (1.0 / 12.0)
    west_open = jnp.broadcast_to(centre(wide_west)[:, :1], (rows, cols)) * (1.0 / 12.0)
    mask_south = wide_mask[6:8, cols : 2 * cols]
    mask_north = wide_mask[8 + rows : 10 + rows, cols : 2 * cols]

    for copy in edge_copies:
        copy.wait_recv()

    def place(level, carry):
        for f in range(tracer_count):
            cells[f, level, 6:8, :] = from_south[f, level] * mask_south
            cells[f, level, 8 + rows : 10 + rows, :] = from_north[f, level] * mask_north
        north_speed[level, 7:8, :] = speed_south[pl.ds(level, 1), :]
        return carry

    lax.fori_loop(0, levels, place, 0, unroll=2)
    for f in range(tracer_count):
        behind = edge_near[1, f]
        ahead = edge_own[0, f]
        west_face[f] = flux(
            speed_west[...] * west_open,
            behind,
            pltpu.roll(behind, cols - 1, 1),
            ahead,
            pltpu.roll(ahead, cols - 1, 1),
            (12.0 * DIFFUSIVITY) * west_open,
        )

    loads[4].wait()
    vert[0] = zero
    vert[levels] = zero

    def advected(level):
        along = east_speed[level] * east_open
        across_north = north_speed[level, 8 : 8 + rows, :] * north_open
        across_south = north_speed[level, 7 : 7 + rows, :] * south_open
        twice = 2 * level
        results = []
        for f in range(tracer_count):
            here = cells[f, level, 8 : 8 + rows, :]
            south1 = cells[f, level, 7 : 7 + rows, :]
            south2 = cells[f, level, 6 : 6 + rows, :]
            north1 = cells[f, level, 9 : 9 + rows, :]
            north2 = cells[f, level, 10 : 10 + rows, :]
            right = pltpu.roll(edge_near[0, f], lax.rem(2 * cols - 2 - twice, cols), 1)
            east2 = jnp.where(lane >= cols - 2, right, pltpu.roll(here, cols - 2, 1))
            east1 = jnp.where(
                lane == cols - 1, pltpu.roll(right, 1, 1), pltpu.roll(here, cols - 1, 1)
            )
            west1 = jnp.where(
                lane == 0,
                pltpu.roll(edge_near[1, f], lax.rem(2 * cols - 1 - twice, cols), 1),
                pltpu.roll(here, 1, 1),
            )
            east_flux = flux(along, west1, here, east1, east2, mix_east)
            west_flux = jnp.where(
                lane == 0,
                pltpu.roll(west_face[f], lax.rem(2 * cols - twice, cols), 1),
                pltpu.roll(east_flux, 1, 1),
            )
            north_flux = flux(across_north, south1, here, north1, north2, mix_north)
            south_flux = flux(across_south, south2, south1, here, north1, mix_south)
            results.append(
                mask * (here - (east_flux - west_flux) - (north_flux - south_flux))
            )
        return results

    mix_east = (12.0 * DIFFUSIVITY) * east_open
    mix_north = (12.0 * DIFFUSIVITY) * north_open
    mix_south = (12.0 * DIFFUSIVITY) * south_open

    half = levels // 2

    def eliminate(step, carry):
        top, top_values, bottom, bottom_values = carry
        low, high = step, levels - 1 - step
        share = jnp.where(step == 0, 1.0, 0.0)
        lower, upper = vert[low], vert[low + 1]
        scale = 1.0 / (1.0 + lower + upper + lower * top)
        top = -upper * scale
        factor[low] = top
        provisional = advected(low)
        top_values = tuple(
            (provisional[f] + share * surface_flux[f] + lower * top_values[f]) * scale
            for f in range(tracer_count)
        )
        for f in range(tracer_count):
            solved[f, low] = top_values[f]
        lower, upper = vert[high], vert[high + 1]
        scale = 1.0 / (1.0 + lower + upper + upper * bottom)
        bottom = -lower * scale
        factor[high] = bottom
        provisional = advected(high)
        bottom_values = tuple(
            (provisional[f] + upper * bottom_values[f]) * scale for f in range(tracer_count)
        )
        for f in range(tracer_count):
            solved[f, high] = bottom_values[f]
        return top, top_values, bottom, bottom_values

    none = (zero,) * tracer_count
    top, top_values, bottom, bottom_values = lax.fori_loop(
        0, half, eliminate, (zero, none, zero, none)
    )
    across = 1.0 / (1.0 - top * bottom)
    up, down = [], []
    for f in range(tracer_count):
        upper_value = (top_values[f] - top * bottom_values[f]) * across
        lower_value = bottom_values[f] - bottom * upper_value
        solved[f, half - 1] = upper_value
        solved[f, half] = lower_value
        up.append(upper_value)
        down.append(lower_value)
    total = (up[0] - up[1]) + (down[0] - down[1])

    def substitute(step, carry):
        up, down, total = carry
        low, high = half - 2 - step, half + 1 + step
        up = tuple(solved[f, low] - factor[low] * up[f] for f in range(tracer_count))
        down = tuple(solved[f, high] - factor[high] * down[f] for f in range(tracer_count))
        for f in range(tracer_count):
            solved[f, low] = up[f]
            solved[f, high] = down[f]
        return up, down, total + ((up[0] - up[1]) + (down[0] - down[1]))

    _, _, total = lax.fori_loop(
        0, half - 1, substitute, (tuple(up), tuple(down), total), unroll=2
    )
    store = pltpu.make_async_copy(solved, new_hbm, local_sem.at[5])
    store.start()

    forcing = mask * total * (1.0 / math.sqrt(2.0 * levels))
    first = centre(inverse) * forcing
    search_own[...] = first
    search[8 : 8 + rows, cols : 2 * cols] = first
    search_copies = sides(SEARCH, search_own, search)
    for copy in search_copies:
        copy.wait_recv()

    def operator(v):
        return (
            diagonal * v
            - east_weight * next_col(v)
            - west_weight * last_col(v)
            - north_weight * next_row(v)
            - south_weight * last_row(v)
        )

    wide_image = operator(search[...])
    wide_second = inverse * wide_image
    image = centre(wide_image)
    second = centre(wide_second)
    second_image = centre(operator(wide_second))

    for k, field in enumerate((forcing, image, second, second_image, first)):
        fields[k] = field
    slot_copies = [
        remote(SLOT, fields, fields_near.at[0], beside(0, 1)),
        remote(SLOT + 1, fields, fields_near.at[1], beside(0, -1)),
    ]

    def rows_sum(v):
        return jnp.sum(v, axis=0, keepdims=True)

    products = (
        rows_sum(forcing * first),
        rows_sum(first * image),
        rows_sum(image * second),
        rows_sum(second * second_image),
    )
    tile_row = lax.broadcasted_iota(jnp.int32, (8, cols), 0)
    sums = jnp.zeros((8, cols), jnp.float32)
    for k, product in enumerate(products):
        sums = jnp.where(tile_row == k, product, sums)
    reduce_copies = []
    for stage in range(3):
        partial[stage] = sums
        copies = [
            remote(
                REDUCE + stage * (GROUP - 1) + k - 1,
                partial.at[stage],
                gathered.at[stage, k - 1],
                partner(stage, k),
            )
            for k in range(1, GROUP)
        ]
        reduce_copies += copies
        for k, copy in enumerate(copies):
            copy.wait_recv()
            sums = sums + gathered[stage, k]
    totals = jnp.sum(sums, axis=1, keepdims=True)
    rho, bend, gap, tail = (totals[k : k + 1] for k in range(4))
    step0 = rho / bend
    rho_next = rho - 2.0 * step0 * bend + step0 * step0 * gap
    ratio = rho_next / rho
    cross = bend - step0 * gap
    inner = bend - 2.0 * step0 * gap + step0 * step0 * tail
    step1 = rho_next / (inner + 2.0 * ratio * cross + ratio * ratio * bend)
    along_first = step0 + step1 * (1.0 + ratio)
    along_second = -step1 * step0

    for copy in slot_copies:
        copy.wait_recv()
    for k, ref in enumerate((fields_near.at[0], fields, fields_near.at[1])):
        placed[0, k * rows : (k + 1) * rows, :] = along_first * ref[4] + along_second * ref[2]
        placed[1, k * rows : (k + 1) * rows, :] = (
            ref[0] - along_first * ref[1] - along_second * ref[3]
        )
    blocks = rows // block_rows
    slots = sea_ref.shape[1]
    for slot in range(slots):
        held = map_ref[0, gx * slots + slot]
        filled = jnp.where(held >= 0, 1.0, 0.0)
        safe = jnp.maximum(held, 0)
        offset = lax.rem(safe // blocks - gx + 1 + n_gx, n_gx)
        target = jnp.minimum(offset * blocks + lax.rem(safe, blocks), 3 * blocks - 1)
        begin = pl.ds(target * block_rows, block_rows)
        sea_ref[0, slot] = filled * placed[0, begin, :]
        slot_ref[0, slot] = filled * placed[1, begin, :]

    for copy in (
        meta_copies + atm_copies + edge_copies + search_copies + slot_copies + reduce_copies
    ):
        copy.wait_send()
    store.wait()


def on_device(
    atm_flux,
    remap_source,
    remap_weight,
    tracers,
    velocity,
    vert_diff,
    ocean_depth,
    surface_term,
    land_mask,
    barotropic_block_map,
):
    n_gy, n_gx = lax.axis_size("gy"), lax.axis_size("gx")
    tracer_count, levels, rows, cols = tracers.shape
    blocks = land_mask.shape[0]
    slots = barotropic_block_map.shape[1] // n_gx
    atm_blocks = atm_flux.shape[1]
    f32 = jnp.float32
    vmem = functools.partial(pltpu.VMEM, dtype=f32)
    in_vmem = pl.BlockSpec(memory_space=pltpu.VMEM)
    in_smem = pl.BlockSpec(memory_space=pltpu.SMEM)
    in_hbm = pl.BlockSpec(memory_space=pltpu.HBM)
    slot_shape = jax.ShapeDtypeStruct((1, slots, rows // blocks, cols), f32)
    return pl.pallas_call(
        functools.partial(kernel, n_gy, n_gx),
        out_shape=(jax.ShapeDtypeStruct(tracers.shape, f32), slot_shape, slot_shape),
        in_specs=[in_smem] * 3 + [in_vmem] * 3 + [in_hbm] * 4,
        out_specs=(in_hbm, in_vmem, in_vmem),
        scratch_shapes=[
            pltpu.VMEM(remap_weight.shape, remap_weight.dtype),
            vmem((tracer_count, levels, rows + 16, cols)),
            vmem((levels, rows, cols)),
            vmem((levels, rows + 8, cols)),
            vmem((levels + 1, rows, cols)),
            vmem((3, rows, cols)),
            vmem((3, rows + 16, 3 * cols)),
            vmem((atm_blocks, tracer_count, cols)),
            vmem((3 * atm_blocks, tracer_count, cols)),
            vmem((tracer_count, levels, 2, cols)),
            vmem((tracer_count, levels, 2, cols)),
            vmem((tracer_count, levels, 2, cols)),
            vmem((tracer_count, levels, 2, cols)),
            vmem((64, cols)),
            vmem((64, cols)),
            vmem((2, tracer_count, rows, cols)),
            vmem((2, tracer_count, rows, cols)),
            vmem((rows, cols)),
            vmem((rows, cols)),
            vmem((tracer_count, rows, cols)),
            vmem((tracer_count, rows, cols)),
            vmem((levels, rows, cols)),
            vmem(tracers.shape),
            vmem((rows, cols)),
            vmem((rows + 16, 3 * cols)),
            vmem((5, rows, cols)),
            vmem((2, 5, rows, cols)),
            vmem((3, 8, cols)),
            vmem((3, GROUP - 1, 8, cols)),
            vmem((2, 3 * rows, cols)),
            pltpu.SemaphoreType.DMA((6,)),
            pltpu.SemaphoreType.DMA((COPIES,)),
            pltpu.SemaphoreType.DMA((COPIES,)),
        ],
        compiler_params=pltpu.CompilerParams(
            collective_id=0, has_side_effects=True, vmem_limit_bytes=48 * 1024 * 1024
        ),
        name="ocean_window",
    )(
        remap_source,
        land_mask,
        barotropic_block_map,
        atm_flux,
        ocean_depth,
        surface_term,
        remap_weight,
        tracers,
        velocity,
        vert_diff,
    )


def solution(mesh):
    return jax.shard_map(
        on_device,
        mesh=mesh,
        in_specs=(
            P("gy", "gx", None, None),
            P("gy", "gx", None),
            P("gy", "gx", None, None, None),
            P(None, None, "gy", "gx"),
            P(None, None, "gy", "gx"),
            P(None, "gy", "gx"),
            P("gy", "gx"),
            P("gy", "gx"),
            P("gy", "gx"),
            P("gy", None),
        ),
        out_specs=(P(None, None, "gy", "gx"), P("gy", "gx", None, None), P("gy", "gx", None, None)),
        check_vma=False,
    )
```

```python
import functools
import math

import jax
import jax.numpy as jnp
from jax import lax
from jax.experimental import pallas as pl
from jax.experimental.pallas import tpu as pltpu
from jax.sharding import PartitionSpec as P

DIFFUSIVITY = 0.1
FLUX_GAIN = 0.5
MESH = pl.DeviceIdType.MESH
GROUP = 8
VMEM_LIMIT = 67043328
SIDES = ((0, 1), (0, -1), (1, 0), (-1, 0), (1, 1), (1, -1), (-1, 1), (-1, -1))
META, ATM, EDGE, SEARCH, SLOT, REDUCE = 0, 8, 10, 18, 26, 28
COPIES = REDUCE + 3 * (GROUP - 1)


def flux(speed, behind, centre, forward, beyond, mixing):
    drop = centre - forward
    return (
        speed * (7.0 * (centre + forward) - (behind + beyond))
        - jnp.abs(speed) * (3.0 * drop + (beyond - behind))
        + mixing * drop
    )


def kernel(
    n_gy,
    n_gx,
    source_ref,
    land_ref,
    map_ref,
    atm_ref,
    depth_ref,
    surface_ref,
    weight_hbm,
    tracer_hbm,
    velocity_hbm,
    vert_hbm,
    new_hbm,
    slots_ref,
    weight,
    cells,
    east_speed,
    north_speed,
    vert,
    meta_own,
    meta,
    atm_own,
    atm_near,
    to_north,
    to_south,
    from_south,
    from_north,
    speed_north,
    speed_south,
    edge_own,
    edge_near,
    speed_east,
    speed_west,
    west_face,
    surface_flux,
    factor,
    scale,
    gain,
    solved,
    search_own,
    search,
    fields,
    fields_near,
    partial,
    gathered,
    placed,
    local_sem,
    send_sem,
    recv_sem,
):
    tracer_count, levels, rows, cols = tracer_hbm.shape
    gy = lax.axis_index("gy")
    gx = lax.axis_index("gx")

    half = levels // 2
    loads = [
        pltpu.make_async_copy(
            tracer_hbm.at[:, part * half : (part + 1) * half],
            cells.at[:, part * half : (part + 1) * half, 8 : 8 + rows, :],
            local_sem.at[part],
        )
        for part in range(2)
    ]
    loads += [
        pltpu.make_async_copy(velocity_hbm.at[0], east_speed, local_sem.at[2]),
        pltpu.make_async_copy(
            velocity_hbm.at[1], north_speed.at[:, 8 : 8 + rows, :], local_sem.at[3]
        ),
        pltpu.make_async_copy(vert_hbm, vert.at[1:levels], local_sem.at[4]),
        pltpu.make_async_copy(weight_hbm, weight, local_sem.at[5]),
    ]
    for load in loads:
        load.start()

    def beside(dy, dx):
        return (lax.rem(gy + dy + n_gy, n_gy), lax.rem(gx + dx + n_gx, n_gx))

    inner_gy, inner_gx = n_gy // GROUP, n_gx // GROUP
    core, column = lax.rem(gy, inner_gy), lax.rem(gx, inner_gx)
    flat = core * inner_gx + column

    def partner(stage, k):
        if stage == 0:
            other = lax.rem(flat + k, GROUP)
            return (gy - core + other // inner_gx, gx - column + lax.rem(other, inner_gx))
        if stage == 1:
            return (gy, lax.rem(gx + k * inner_gx, n_gx))
        return (lax.rem(gy + k * inner_gy, n_gy), gx)

    barrier = pltpu.get_barrier_semaphore()
    peers = [beside(dy, dx) for dy, dx in SIDES]
    peers += [partner(stage, k) for stage in range(3) for k in range(1, GROUP)]
    for peer in peers:
        pl.semaphore_signal(barrier, inc=1, device_id=peer, device_id_type=MESH)

    def remote(index, src, dst, device):
        copy = pltpu.make_async_remote_copy(
            src_ref=src,
            dst_ref=dst,
            send_sem=send_sem.at[index],
            recv_sem=recv_sem.at[index],
            device_id=device,
            device_id_type=MESH,
        )
        copy.start()
        return copy

    def sides(first, own, padded):
        lead = (slice(None),) * (len(own.shape) - 2)
        source_rows = {0: slice(0, rows), 1: slice(rows - 8, rows), -1: slice(0, 8)}
        target_rows = {0: slice(8, 8 + rows), 1: slice(0, 8), -1: slice(8 + rows, 16 + rows)}
        target_cols = {
            0: slice(cols, 2 * cols),
            1: slice(0, cols),
            -1: slice(2 * cols, 3 * cols),
        }
        return [
            remote(
                first + k,
                own.at[lead + (source_rows[dy],)],
                padded.at[lead + (target_rows[dy], target_cols[dx])],
                beside(dy, dx),
            )
            for k, (dy, dx) in enumerate(SIDES)
        ]

    row = lax.broadcasted_iota(jnp.int32, (rows, cols), 0)
    lane = lax.broadcasted_iota(jnp.int32, (rows, cols), 1)
    block_rows = rows // land_ref.shape[1]
    mask = jnp.zeros((rows, cols), jnp.float32)
    for block in range(land_ref.shape[1]):
        wet = land_ref[0, block].astype(jnp.float32)
        mask = jnp.where(row // block_rows == block, wet, mask)
    meta_own[0] = mask
    meta_own[1] = depth_ref[...]
    meta_own[2] = surface_ref[...]
    for k in range(3):
        meta[k, 8 : 8 + rows, cols : 2 * cols] = meta_own[k]
    atm_own[...] = atm_ref[0].astype(jnp.float32)
    blocks_near = atm_own.shape[0]
    atm_near[blocks_near : 2 * blocks_near] = atm_own[...]

    zero = jnp.zeros((rows, cols), jnp.float32)
    pair = lane // 2

    def pack(level, packed):
        packed = list(packed)
        here = pair == level
        for f in range(tracer_count):
            values = cells[f, level, 8 : 8 + rows, :] * mask
            cells[f, level, 8 : 8 + rows, :] = values
            to_north[level, f] = values[rows - 2 :]
            to_south[level, f] = values[:2]
            packed[2 * f] = jnp.where(here, pltpu.roll(values, 2 * level, 1), packed[2 * f])
            packed[2 * f + 1] = jnp.where(
                here, pltpu.roll(values, lax.rem(2 * level + 2, cols), 1), packed[2 * f + 1]
            )
        return tuple(packed)

    def row_copies(part):
        span = slice(part * half, (part + 1) * half)
        return [
            remote(EDGE + 2 * part, to_north.at[span], from_south.at[span], beside(1, 0)),
            remote(EDGE + 2 * part + 1, to_south.at[span], from_north.at[span], beside(-1, 0)),
        ]

    loads[0].wait()
    packed = lax.fori_loop(0, half, pack, (zero,) * (2 * tracer_count), unroll=4)
    pl.semaphore_wait(barrier, len(peers))
    near_copies = [row_copies(0)]
    meta_copies = sides(META, meta_own, meta)
    atm_copies = [
        remote(ATM, atm_own, atm_near.at[0:blocks_near], beside(0, 1)),
        remote(ATM + 1, atm_own, atm_near.at[2 * blocks_near : 3 * blocks_near], beside(0, -1)),
    ]
    loads[1].wait()
    packed = lax.fori_loop(half, levels, pack, packed, unroll=4)
    near_copies.append(row_copies(1))
    for f in range(tracer_count):
        edge_own[0, f] = packed[2 * f]
        edge_own[1, f] = packed[2 * f + 1]
    edge_copies = [
        remote(EDGE + 4, edge_own.at[0], edge_near.at[0], beside(0, -1)),
        remote(EDGE + 5, edge_own.at[1], edge_near.at[1], beside(0, 1)),
    ]

    loads[2].wait()
    loads[3].wait()

    def pack_speed(level, packed):
        speed_north[pl.ds(level, 1), :] = north_speed[level, 7 + rows : 8 + rows, :]
        return jnp.where(
            pair == level,
            pltpu.roll(east_speed[level], lax.rem(2 * level + 1, cols), 1),
            packed,
        )

    speed_east[...] = lax.fori_loop(0, levels, pack_speed, zero, unroll=2)
    edge_copies += [
        remote(EDGE + 6, speed_north, speed_south, beside(1, 0)),
        remote(EDGE + 7, speed_east, speed_west, beside(0, 1)),
    ]

    loads[4].wait()
    vert[0] = zero
    vert[levels] = zero

    def eliminate(step, carry):
        top, bottom = carry
        low, high = step, levels - 1 - step
        lower, upper = vert[low], vert[low + 1]
        share = 1.0 / (1.0 + lower + upper + lower * top)
        top = -upper * share
        factor[low] = top
        scale[low] = share
        gain[low] = lower * share
        lower, upper = vert[high], vert[high + 1]
        share = 1.0 / (1.0 + lower + upper + upper * bottom)
        bottom = -lower * share
        factor[high] = bottom
        scale[high] = share
        gain[high] = upper * share
        return top, bottom

    top, bottom = lax.fori_loop(0, half, eliminate, (zero, zero))

    loads[5].wait()
    for copy in atm_copies:
        copy.wait_recv()

    def remap(r, carry):
        total = jnp.zeros((tracer_count, cols), jnp.float32)
        for k in range(weight.shape[2]):
            picked = atm_near[source_ref[0, k, r]].astype(jnp.bfloat16)
            total += lax.dot_general(
                picked,
                weight[r, 0, k],
                (((1,), (1,)), ((), ())),
                preferred_element_type=jnp.float32,
            )
        for f in range(tracer_count):
            surface_flux[f, pl.ds(r, 1), :] = total[f : f + 1]
        return carry

    lax.fori_loop(0, rows, remap, 0, unroll=4)
    for f in range(tracer_count):
        surface_flux[f] = FLUX_GAIN * mask * surface_flux[f]

    for copy in meta_copies:
        copy.wait_recv()
    height, width = search.shape
    wide_row = lax.broadcasted_iota(jnp.int32, (height, width), 0)
    below = jnp.where(gy > 0, 1.0, 0.0)
    above = jnp.where(gy < n_gy - 1, 1.0, 0.0)
    inside = jnp.where(wide_row < 8, below, jnp.where(wide_row >= 8 + rows, above, 1.0))
    wide_mask = meta[0] * inside
    depth = meta[1]

    def next_col(v):
        return pltpu.roll(v, width - 1, 1)

    def last_col(v):
        return pltpu.roll(v, 1, 1)

    def next_row(v):
        return pltpu.roll(v, height - 1, 0)

    def last_row(v):
        return pltpu.roll(v, 1, 0)

    wide_east = wide_mask * next_col(wide_mask)
    wide_north = wide_mask * next_row(wide_mask)
    east_weight = wide_east * (depth + next_col(depth)) * 0.5
    north_weight = wide_north * (depth + next_row(depth)) * 0.5
    west_weight = last_col(east_weight)
    south_weight = last_row(north_weight)
    diagonal = (
        wide_mask * meta[2]
        + (1.0 - wide_mask)
        + east_weight
        + west_weight
        + north_weight
        + south_weight
    )
    inverse = 1.0 / diagonal
    wide_south = last_row(wide_north)
    wide_west = last_col(wide_east)

    def centre(v):
        return v[8 : 8 + rows, cols : 2 * cols]

    east_open = centre(wide_east) * (1.0 / 12.0)
    north_open = centre(wide_north) * (1.0 / 12.0)
    south_open = centre(wide_south) * (1.0 / 12.0)
    west_open = jnp.broadcast_to(centre(wide_west)[:, :1], (rows, cols)) * (1.0 / 12.0)
    mask_south = wide_mask[6:8, cols : 2 * cols]
    mask_north = wide_mask[8 + rows : 10 + rows, cols : 2 * cols]

    for copy in edge_copies:
        copy.wait_recv()

    for f in range(tracer_count):
        behind = edge_near[1, f]
        ahead = edge_own[0, f]
        west_face[f] = flux(
            speed_west[...] * west_open,
            behind,
            pltpu.roll(behind, cols - 1, 1),
            ahead,
            pltpu.roll(ahead, cols - 1, 1),
            (12.0 * DIFFUSIVITY) * west_open,
        )

    def advected(level):
        along = east_speed[level] * east_open
        across_north = north_speed[level, 8 : 8 + rows, :] * north_open
        across_south = north_speed[level, 7 : 7 + rows, :] * south_open
        twice = 2 * level
        results = []
        for f in range(tracer_count):
            here = cells[f, level, 8 : 8 + rows, :]
            south1 = cells[f, level, 7 : 7 + rows, :]
            south2 = cells[f, level, 6 : 6 + rows, :]
            north1 = cells[f, level, 9 : 9 + rows, :]
            north2 = cells[f, level, 10 : 10 + rows, :]
            right = pltpu.roll(edge_near[0, f], lax.rem(2 * cols - 2 - twice, cols), 1)
            east2 = jnp.where(lane >= cols - 2, right, pltpu.roll(here, cols - 2, 1))
            east1 = jnp.where(
                lane == cols - 1, pltpu.roll(right, 1, 1), pltpu.roll(here, cols - 1, 1)
            )
            west1 = jnp.where(
                lane == 0,
                pltpu.roll(edge_near[1, f], lax.rem(2 * cols - 1 - twice, cols), 1),
                pltpu.roll(here, 1, 1),
            )
            east_flux = flux(along, west1, here, east1, east2, mix_east)
            west_flux = jnp.where(
                lane == 0,
                pltpu.roll(west_face[f], lax.rem(2 * cols - twice, cols), 1),
                pltpu.roll(east_flux, 1, 1),
            )
            north_flux = flux(across_north, south1, here, north1, north2, mix_north)
            south_flux = flux(across_south, south2, south1, here, north1, mix_south)
            results.append(
                mask * (here - (east_flux - west_flux) - (north_flux - south_flux))
            )
        return results

    mix_east = (12.0 * DIFFUSIVITY) * east_open
    mix_north = (12.0 * DIFFUSIVITY) * north_open
    mix_south = (12.0 * DIFFUSIVITY) * south_open

    def advect(level, total):
        for f in range(tracer_count):
            cells[f, level, 6:8, :] = from_south[level, f] * mask_south
            cells[f, level, 8 + rows : 10 + rows, :] = from_north[level, f] * mask_north
        north_speed[level, 7:8, :] = speed_south[pl.ds(level, 1), :]
        provisional = advected(level)
        for f in range(tracer_count):
            solved[f, level] = provisional[f]
        return total + (provisional[0] - provisional[1])

    total = surface_flux[0] - surface_flux[1]
    for part in range(2):
        for copy in near_copies[part]:
            copy.wait_recv()
        total = lax.fori_loop(part * half, (part + 1) * half, advect, total)
    for f in range(tracer_count):
        solved[f, 0] = solved[f, 0] + surface_flux[f]

    forcing = mask * total * (1.0 / math.sqrt(2.0 * levels))
    first = centre(inverse) * forcing
    search_own[...] = first
    search[8 : 8 + rows, cols : 2 * cols] = first
    search_copies = sides(SEARCH, search_own, search)

    def inward(step, carry):
        low, high = step, levels - 1 - step
        values = []
        for level, before in ((low, carry[0]), (high, carry[1])):
            value = tuple(
                solved[f, level] * scale[level] + gain[level] * before[f]
                for f in range(tracer_count)
            )
            for f in range(tracer_count):
                solved[f, level] = value[f]
            values.append(value)
        return tuple(values)

    none = (zero,) * tracer_count
    top_values, bottom_values = lax.fori_loop(0, half, inward, (none, none), unroll=2)
    across = 1.0 / (1.0 - top * bottom)
    up, down = [], []
    for f in range(tracer_count):
        upper_value = (top_values[f] - top * bottom_values[f]) * across
        lower_value = bottom_values[f] - bottom * upper_value
        solved[f, half - 1] = upper_value
        solved[f, half] = lower_value
        up.append(upper_value)
        down.append(lower_value)

    def outward(step, carry):
        values = []
        for level, before in ((half - 2 - step, carry[0]), (half + 1 + step, carry[1])):
            value = tuple(
                solved[f, level] - factor[level] * before[f] for f in range(tracer_count)
            )
            for f in range(tracer_count):
                solved[f, level] = value[f]
            values.append(value)
        return tuple(values)

    lax.fori_loop(0, half - 1, outward, (tuple(up), tuple(down)), unroll=2)
    store = pltpu.make_async_copy(solved, new_hbm, local_sem.at[6])
    store.start()

    for copy in search_copies:
        copy.wait_recv()

    def operator(v):
        return (
            diagonal * v
            - east_weight * next_col(v)
            - west_weight * last_col(v)
            - north_weight * next_row(v)
            - south_weight * last_row(v)
        )

    wide_image = operator(search[...])
    wide_second = inverse * wide_image
    image = centre(wide_image)
    second = centre(wide_second)
    second_image = centre(operator(wide_second))

    for k, field in enumerate((forcing, image, second, second_image)):
        fields[k] = field

    def rows_sum(v):
        return jnp.sum(v, axis=0, keepdims=True)

    products = (
        rows_sum(forcing * first),
        rows_sum(first * image),
        rows_sum(image * second),
        rows_sum(second * second_image),
    )
    tile_row = lax.broadcasted_iota(jnp.int32, (8, cols), 0)
    sums = jnp.zeros((8, cols), jnp.float32)
    for k, product in enumerate(products):
        sums = jnp.where(tile_row == k, product, sums)
    sums = jnp.sum(sums, axis=1, keepdims=True)
    place = lax.broadcasted_iota(jnp.int32, (1, cols), 1)
    line = jnp.zeros((1, cols), jnp.float32)
    for k in range(4):
        line = jnp.where(place == k, sums[k : k + 1], line)
    reduce_copies = []
    slot_copies = []
    for stage in range(3):
        partial[stage] = line
        copies = [
            remote(
                REDUCE + stage * (GROUP - 1) + k - 1,
                partial.at[stage],
                gathered.at[stage, k - 1],
                partner(stage, k),
            )
            for k in range(1, GROUP)
        ]
        reduce_copies += copies
        if stage == 0:
            slot_copies = [
                remote(SLOT, fields, fields_near.at[0], beside(0, 1)),
                remote(SLOT + 1, fields, fields_near.at[1], beside(0, -1)),
            ]
        for k, copy in enumerate(copies):
            copy.wait_recv()
            line = line + gathered[stage, k]
    rho, bend, gap, tail = (
        jnp.sum(jnp.where(place == k, line, 0.0), axis=1, keepdims=True) for k in range(4)
    )
    step0 = rho / bend
    rho_next = rho - 2.0 * step0 * bend + step0 * step0 * gap
    ratio = rho_next / rho
    cross = bend - step0 * gap
    inner = bend - 2.0 * step0 * gap + step0 * step0 * tail
    step1 = rho_next / (inner + 2.0 * ratio * cross + ratio * ratio * bend)
    along_first = step0 + step1 * (1.0 + ratio)
    along_second = -step1 * step0

    for copy in slot_copies:
        copy.wait_recv()
    for k, ref in enumerate((fields_near.at[0], fields, fields_near.at[1])):
        nearby = search[8 : 8 + rows, k * cols : (k + 1) * cols]
        placed[0, k * rows : (k + 1) * rows, :] = along_first * nearby + along_second * ref[2]
        placed[1, k * rows : (k + 1) * rows, :] = (
            ref[0] - along_first * ref[1] - along_second * ref[3]
        )
    blocks = rows // block_rows
    slots = slots_ref.shape[1]
    for slot in range(slots):
        held = map_ref[0, gx * slots + slot]
        filled = jnp.where(held >= 0, 1.0, 0.0)
        safe = jnp.maximum(held, 0)
        offset = lax.rem(safe // blocks - gx + 1 + n_gx, n_gx)
        target = jnp.minimum(offset * blocks + lax.rem(safe, blocks), 3 * blocks - 1)
        begin = pl.ds(target * block_rows, block_rows)
        slots_ref[0, slot] = filled * placed[0, begin, :]
        slots_ref[1, slot] = filled * placed[1, begin, :]

    for copy in (
        meta_copies
        + atm_copies
        + near_copies[0]
        + near_copies[1]
        + edge_copies
        + search_copies + slot_copies + reduce_copies
    ):
        copy.wait_send()
    store.wait()


def on_device(
    atm_flux,
    remap_source,
    remap_weight,
    tracers,
    velocity,
    vert_diff,
    ocean_depth,
    surface_term,
    land_mask,
    barotropic_block_map,
):
    n_gy, n_gx = lax.axis_size("gy"), lax.axis_size("gx")
    tracer_count, levels, rows, cols = tracers.shape
    blocks = land_mask.shape[0]
    slots = barotropic_block_map.shape[1] // n_gx
    atm_blocks = atm_flux.shape[1]
    f32 = jnp.float32
    vmem = functools.partial(pltpu.VMEM, dtype=f32)
    in_vmem = pl.BlockSpec(memory_space=pltpu.VMEM)
    in_smem = pl.BlockSpec(memory_space=pltpu.SMEM)
    in_hbm = pl.BlockSpec(memory_space=pltpu.HBM)
    slot_shape = jax.ShapeDtypeStruct((2, slots, rows // blocks, cols), f32)
    new_tracers, in_slots = pl.pallas_call(
        functools.partial(kernel, n_gy, n_gx),
        out_shape=(jax.ShapeDtypeStruct(tracers.shape, f32), slot_shape),
        in_specs=[in_smem] * 3 + [in_vmem] * 3 + [in_hbm] * 4,
        out_specs=(in_hbm, in_vmem),
        scratch_shapes=[
            pltpu.VMEM(remap_weight.shape, remap_weight.dtype),
            vmem((tracer_count, levels, rows + 16, cols)),
            vmem((levels, rows, cols)),
            vmem((levels, rows + 8, cols)),
            vmem((levels + 1, rows, cols)),
            vmem((3, rows, cols)),
            vmem((3, rows + 16, 3 * cols)),
            vmem((atm_blocks, tracer_count, cols)),
            vmem((3 * atm_blocks, tracer_count, cols)),
            vmem((levels, tracer_count, 2, cols)),
            vmem((levels, tracer_count, 2, cols)),
            vmem((levels, tracer_count, 2, cols)),
            vmem((levels, tracer_count, 2, cols)),
            vmem((64, cols)),
            vmem((64, cols)),
            vmem((2, tracer_count, rows, cols)),
            vmem((2, tracer_count, rows, cols)),
            vmem((rows, cols)),
            vmem((rows, cols)),
            vmem((tracer_count, rows, cols)),
            vmem((tracer_count, rows, cols)),
            vmem((levels, rows, cols)),
            vmem((levels, rows, cols)),
            vmem((levels, rows, cols)),
            vmem(tracers.shape),
            vmem((rows, cols)),
            vmem((rows + 16, 3 * cols)),
            vmem((4, rows, cols)),
            vmem((2, 4, rows, cols)),
            vmem((3, 1, cols)),
            vmem((3, GROUP - 1, 1, cols)),
            vmem((2, 3 * rows, cols)),
            pltpu.SemaphoreType.DMA((7,)),
            pltpu.SemaphoreType.DMA((COPIES,)),
            pltpu.SemaphoreType.DMA((COPIES,)),
        ],
        compiler_params=pltpu.CompilerParams(
            collective_id=0, has_side_effects=True, vmem_limit_bytes=VMEM_LIMIT
        ),
        name="ocean_window",
    )(
        jnp.transpose(remap_source, (1, 2, 0)),
        land_mask.T,
        barotropic_block_map,
        atm_flux,
        ocean_depth,
        surface_term,
        remap_weight,
        tracers,
        velocity,
        vert_diff,
    )
    return new_tracers, in_slots[:1], in_slots[1:]


def solution(mesh):
    return jax.shard_map(
        on_device,
        mesh=mesh,
        in_specs=(
            P("gy", "gx", None, None),
            P("gy", "gx", None),
            P("gy", "gx", None, None, None),
            P(None, None, "gy", "gx"),
            P(None, None, "gy", "gx"),
            P(None, "gy", "gx"),
            P("gy", "gx"),
            P("gy", "gx"),
            P("gy", "gx"),
            P("gy", None),
        ),
        out_specs=(P(None, None, "gy", "gx"), P("gy", "gx", None, None), P("gy", "gx", None, None)),
        check_vma=False,
    )
```

```python
import functools
import math

import jax
import jax.numpy as jnp
from jax import lax
from jax.experimental import pallas as pl
from jax.experimental.pallas import tpu as pltpu
from jax.sharding import PartitionSpec as P

DIFFUSIVITY = 0.1
FLUX_GAIN = 0.5
MESH = pl.DeviceIdType.MESH
GROUP = 8
VMEM_LIMIT = 67043328
SIDES = ((0, 1), (0, -1), (1, 0), (-1, 0), (1, 1), (1, -1), (-1, 1), (-1, -1))
META, ATM, EDGE, SEARCH, SLOT, REDUCE = 0, 8, 10, 18, 26, 28
COPIES = REDUCE + 3 * (GROUP - 1)


def flux(speed, behind, centre, forward, beyond, mixing):
    drop = centre - forward
    return (
        speed * (7.0 * (centre + forward) - (behind + beyond))
        - jnp.abs(speed) * (3.0 * drop + (beyond - behind))
        + mixing * drop
    )


def kernel(
    n_gy,
    n_gx,
    source_ref,
    land_ref,
    map_ref,
    atm_hbm,
    depth_hbm,
    surface_hbm,
    weight_hbm,
    tracer_hbm,
    velocity_hbm,
    vert_hbm,
    new_hbm,
    slots_ref,
    weight,
    cells,
    east_speed,
    north_speed,
    vert,
    meta_own,
    meta,
    atm_raw,
    atm_own,
    atm_near,
    to_north,
    to_south,
    from_south,
    from_north,
    speed_north,
    speed_south,
    edge_own,
    edge_near,
    speed_east,
    speed_west,
    west_face,
    beyond,
    surface_flux,
    factor,
    scale,
    gain,
    solved,
    search_own,
    search,
    fields,
    fields_near,
    partial,
    gathered,
    placed,
    local_sem,
    send_sem,
    recv_sem,
):
    tracer_count, levels, rows, cols = tracer_hbm.shape
    gy = lax.axis_index("gy")
    gx = lax.axis_index("gx")

    half = levels // 2
    loads = [
        pltpu.make_async_copy(
            tracer_hbm.at[:, part * half : (part + 1) * half],
            cells.at[:, part * half : (part + 1) * half, 8 : 8 + rows, :],
            local_sem.at[part],
        )
        for part in range(2)
    ]
    loads += [
        pltpu.make_async_copy(velocity_hbm.at[0], east_speed, local_sem.at[2]),
        pltpu.make_async_copy(
            velocity_hbm.at[1], north_speed.at[:, 8 : 8 + rows, :], local_sem.at[3]
        ),
        pltpu.make_async_copy(vert_hbm, vert.at[1:levels], local_sem.at[4]),
        pltpu.make_async_copy(weight_hbm, weight, local_sem.at[5]),
    ]
    small = [
        pltpu.make_async_copy(depth_hbm, meta_own.at[1], local_sem.at[7]),
        pltpu.make_async_copy(surface_hbm, meta_own.at[2], local_sem.at[8]),
        pltpu.make_async_copy(atm_hbm, atm_raw, local_sem.at[9]),
    ]
    for load in small + loads:
        load.start()

    def beside(dy, dx):
        return (lax.rem(gy + dy + n_gy, n_gy), lax.rem(gx + dx + n_gx, n_gx))

    inner_gy, inner_gx = n_gy // GROUP, n_gx // GROUP
    core, column = lax.rem(gy, inner_gy), lax.rem(gx, inner_gx)
    flat = core * inner_gx + column

    def partner(stage, k):
        if stage == 0:
            other = lax.rem(flat + k, GROUP)
            return (gy - core + other // inner_gx, gx - column + lax.rem(other, inner_gx))
        if stage == 1:
            return (gy, lax.rem(gx + k * inner_gx, n_gx))
        return (lax.rem(gy + k * inner_gy, n_gy), gx)

    barrier = pltpu.get_barrier_semaphore()
    peers = [beside(dy, dx) for dy, dx in SIDES]
    peers += [partner(stage, k) for stage in range(3) for k in range(1, GROUP)]
    for peer in peers:
        pl.semaphore_signal(barrier, inc=1, device_id=peer, device_id_type=MESH)

    def remote(index, src, dst, device):
        copy = pltpu.make_async_remote_copy(
            src_ref=src,
            dst_ref=dst,
            send_sem=send_sem.at[index],
            recv_sem=recv_sem.at[index],
            device_id=device,
            device_id_type=MESH,
        )
        copy.start()
        return copy

    def sides(first, own, padded):
        lead = (slice(None),) * (len(own.shape) - 2)
        source_rows = {0: slice(0, rows), 1: slice(rows - 8, rows), -1: slice(0, 8)}
        target_rows = {0: slice(8, 8 + rows), 1: slice(0, 8), -1: slice(8 + rows, 16 + rows)}
        target_cols = {
            0: slice(cols, 2 * cols),
            1: slice(0, cols),
            -1: slice(2 * cols, 3 * cols),
        }
        return [
            remote(
                first + k,
                own.at[lead + (source_rows[dy],)],
                padded.at[lead + (target_rows[dy], target_cols[dx])],
                beside(dy, dx),
            )
            for k, (dy, dx) in enumerate(SIDES)
        ]

    row = lax.broadcasted_iota(jnp.int32, (rows, cols), 0)
    lane = lax.broadcasted_iota(jnp.int32, (rows, cols), 1)
    block_rows = rows // land_ref.shape[1]
    mask = jnp.zeros((rows, cols), jnp.float32)
    for block in range(land_ref.shape[1]):
        wet = land_ref[0, block].astype(jnp.float32)
        mask = jnp.where(row // block_rows == block, wet, mask)
    meta_own[0] = mask
    for load in small:
        load.wait()
    for k in range(3):
        meta[k, 8 : 8 + rows, cols : 2 * cols] = meta_own[k]
    atm_own[...] = atm_raw[0].astype(jnp.float32)
    blocks_near = atm_own.shape[0]
    atm_near[blocks_near : 2 * blocks_near] = atm_own[...]

    zero = jnp.zeros((rows, cols), jnp.float32)
    group = lane // 4

    def pack(part, level, packed):
        index = level - part * half
        kept = []
        for f in range(tracer_count):
            values = cells[f, level, 8 : 8 + rows, :] * mask
            cells[f, level, 8 : 8 + rows, :] = values
            to_north[level, f] = values[rows - 2 :]
            to_south[level, f] = values[:2]
            turned = pltpu.roll(values, 4 * index + 2, 1)
            kept.append(jnp.where(group == index, turned, packed[f]))
        return tuple(kept)

    def row_copies(part):
        span = slice(part * half, (part + 1) * half)
        return [
            remote(EDGE + 2 * part, to_north.at[span], from_south.at[span], beside(1, 0)),
            remote(EDGE + 2 * part + 1, to_south.at[span], from_north.at[span], beside(-1, 0)),
        ]

    loads[0].wait()
    packed = lax.fori_loop(
        0, half, functools.partial(pack, 0), (zero,) * tracer_count, unroll=4
    )
    for f in range(tracer_count):
        edge_own[0, f] = packed[f]
    pl.semaphore_wait(barrier, len(peers))
    near_copies = [row_copies(0)]
    meta_copies = sides(META, meta_own, meta)
    atm_copies = [
        remote(ATM, atm_own, atm_near.at[0:blocks_near], beside(0, 1)),
        remote(ATM + 1, atm_own, atm_near.at[2 * blocks_near : 3 * blocks_near], beside(0, -1)),
    ]
    loads[1].wait()
    packed = lax.fori_loop(
        half, levels, functools.partial(pack, 1), (zero,) * tracer_count, unroll=4
    )
    near_copies.append(row_copies(1))
    for f in range(tracer_count):
        edge_own[1, f] = packed[f]
    edge_copies = [
        remote(EDGE + 4, edge_own, edge_near.at[0], beside(0, -1)),
        remote(EDGE + 5, edge_own, edge_near.at[1], beside(0, 1)),
    ]

    loads[2].wait()
    loads[3].wait()

    def pack_speed(part, level, packed):
        index = level - part * half
        speed_north[pl.ds(level, 1), :] = north_speed[level, 7 + rows : 8 + rows, :]
        turned = pltpu.roll(east_speed[level], 4 * index + 1, 1)
        return jnp.where(group == index, turned, packed)

    for part in range(2):
        speed_east[part] = lax.fori_loop(
            part * half, (part + 1) * half, functools.partial(pack_speed, part), zero, unroll=4
        )
    edge_copies += [
        remote(EDGE + 6, speed_north, speed_south, beside(1, 0)),
        remote(EDGE + 7, speed_east, speed_west, beside(0, 1)),
    ]

    loads[4].wait()
    vert[0] = zero
    vert[levels] = zero

    def eliminate(step, carry):
        top, bottom = carry
        low, high = step, levels - 1 - step
        lower, upper = vert[low], vert[low + 1]
        share = 1.0 / (1.0 + lower + upper + lower * top)
        top = -upper * share
        factor[low] = top
        scale[low] = share
        gain[low] = lower * share
        lower, upper = vert[high], vert[high + 1]
        share = 1.0 / (1.0 + lower + upper + upper * bottom)
        bottom = -lower * share
        factor[high] = bottom
        scale[high] = share
        gain[high] = upper * share
        return top, bottom

    top, bottom = lax.fori_loop(0, half, eliminate, (zero, zero))

    loads[5].wait()
    for copy in atm_copies:
        copy.wait_recv()

    def remap(r, carry):
        total = jnp.zeros((tracer_count, cols), jnp.float32)
        for k in range(weight.shape[2]):
            picked = atm_near[source_ref[0, k, r]].astype(jnp.bfloat16)
            total += lax.dot_general(
                picked,
                weight[r, 0, k],
                (((1,), (1,)), ((), ())),
                preferred_element_type=jnp.float32,
            )
        for f in range(tracer_count):
            surface_flux[f, pl.ds(r, 1), :] = total[f : f + 1]
        return carry

    lax.fori_loop(0, rows, remap, 0, unroll=4)
    for f in range(tracer_count):
        surface_flux[f] = FLUX_GAIN * mask * surface_flux[f]

    for copy in meta_copies:
        copy.wait_recv()
    height, width = search.shape
    wide_row = lax.broadcasted_iota(jnp.int32, (height, width), 0)
    below = jnp.where(gy > 0, 1.0, 0.0)
    above = jnp.where(gy < n_gy - 1, 1.0, 0.0)
    inside = jnp.where(wide_row < 8, below, jnp.where(wide_row >= 8 + rows, above, 1.0))
    wide_mask = meta[0] * inside
    depth = meta[1]

    def next_col(v):
        return pltpu.roll(v, width - 1, 1)

    def last_col(v):
        return pltpu.roll(v, 1, 1)

    def next_row(v):
        return pltpu.roll(v, height - 1, 0)

    def last_row(v):
        return pltpu.roll(v, 1, 0)

    wide_east = wide_mask * next_col(wide_mask)
    wide_north = wide_mask * next_row(wide_mask)
    east_weight = wide_east * (depth + next_col(depth)) * 0.5
    north_weight = wide_north * (depth + next_row(depth)) * 0.5
    west_weight = last_col(east_weight)
    south_weight = last_row(north_weight)
    diagonal = (
        wide_mask * meta[2]
        + (1.0 - wide_mask)
        + east_weight
        + west_weight
        + north_weight
        + south_weight
    )
    inverse = 1.0 / diagonal
    wide_south = last_row(wide_north)
    wide_west = last_col(wide_east)

    def centre(v):
        return v[8 : 8 + rows, cols : 2 * cols]

    east_open = centre(wide_east) * (1.0 / 12.0)
    north_open = centre(wide_north) * (1.0 / 12.0)
    south_open = centre(wide_south) * (1.0 / 12.0)
    west_open = jnp.broadcast_to(centre(wide_west)[:, :1], (rows, cols)) * (1.0 / 12.0)
    mask_south = wide_mask[6:8, cols : 2 * cols]
    mask_north = wide_mask[8 + rows : 10 + rows, cols : 2 * cols]

    for copy in edge_copies:
        copy.wait_recv()

    for part in range(2):
        for f in range(tracer_count):
            behind = edge_near[1, part, f]
            ahead = edge_own[part, f]
            west_face[part, f] = flux(
                speed_west[part] * west_open,
                behind,
                pltpu.roll(behind, cols - 1, 1),
                pltpu.roll(ahead, cols - 2, 1),
                pltpu.roll(ahead, cols - 3, 1),
                (12.0 * DIFFUSIVITY) * west_open,
            )
            beyond[part, f] = jnp.where(lane % 4 < 2, behind, edge_near[0, part, f])

    def coefficients(speed, mixing):
        size = jnp.abs(speed)
        common, tilt = 7.0 * speed, 3.0 * size - mixing
        return size - speed, common - tilt, common + tilt, size + speed

    def advected(part, level):
        back_e, centre_e, next_e, far_e = coefficients(east_speed[level] * east_open, mix_east)
        back_n, centre_n, next_n, far_n = coefficients(
            north_speed[level, 8 : 8 + rows, :] * north_open, mix_north
        )
        back_s, centre_s, next_s, far_s = coefficients(
            north_speed[level, 7 : 7 + rows, :] * south_open, mix_south
        )
        at_here = centre_n - next_s
        at_north = next_n + far_s
        at_south = back_n - centre_s
        turn = 4 * (level - part * half)
        results = []
        for f in range(tracer_count):
            here = cells[f, level, 8 : 8 + rows, :]
            south1 = cells[f, level, 7 : 7 + rows, :]
            south2 = cells[f, level, 6 : 6 + rows, :]
            north1 = cells[f, level, 9 : 9 + rows, :]
            north2 = cells[f, level, 10 : 10 + rows, :]
            outer = pltpu.roll(beyond[part, f], lax.rem(2 * cols - 2 - turn, cols), 1)
            east2 = pltpu.roll(jnp.where(lane < 2, outer, here), cols - 2, 1)
            east1 = pltpu.roll(jnp.where(lane < 1, outer, here), cols - 1, 1)
            west1 = pltpu.roll(jnp.where(lane == cols - 1, outer, here), 1, 1)
            east_flux = (centre_e * here + next_e * east1) + (back_e * west1 - far_e * east2)
            west_flux = jnp.where(
                lane == 0,
                pltpu.roll(west_face[part, f], lax.rem(cols - turn, cols), 1),
                pltpu.roll(east_flux, 1, 1),
            )
            spread = (at_here * here + at_north * north1) + (
                at_south * south1 - (far_n * north2 + back_s * south2)
            )
            results.append(mask * (here - (east_flux - west_flux) - spread))
        return results

    mix_east = (12.0 * DIFFUSIVITY) * east_open
    mix_north = (12.0 * DIFFUSIVITY) * north_open
    mix_south = (12.0 * DIFFUSIVITY) * south_open

    def put(level, carry):
        for f in range(tracer_count):
            cells[f, level, 6:8, :] = from_south[level, f] * mask_south
            cells[f, level, 8 + rows : 10 + rows, :] = from_north[level, f] * mask_north
        north_speed[level, 7:8, :] = speed_south[pl.ds(level, 1), :]
        return carry

    def advect(part, level, total):
        provisional = advected(part, level)
        for f in range(tracer_count):
            solved[f, level] = provisional[f]
        return total + (provisional[0] - provisional[1])

    total = surface_flux[0] - surface_flux[1]
    for part in range(2):
        for copy in near_copies[part]:
            copy.wait_recv()
        lax.fori_loop(part * half, (part + 1) * half, put, 0, unroll=4)
        total = lax.fori_loop(
            part * half, (part + 1) * half, functools.partial(advect, part), total, unroll=1
        )
    for f in range(tracer_count):
        solved[f, 0] = solved[f, 0] + surface_flux[f]

    forcing = mask * total * (1.0 / math.sqrt(2.0 * levels))
    first = centre(inverse) * forcing
    search_own[...] = first
    search[8 : 8 + rows, cols : 2 * cols] = first
    search_copies = sides(SEARCH, search_own, search)

    def inward(step, carry):
        low, high = step, levels - 1 - step
        values = []
        for level, before in ((low, carry[0]), (high, carry[1])):
            value = tuple(
                solved[f, level] * scale[level] + gain[level] * before[f]
                for f in range(tracer_count)
            )
            for f in range(tracer_count):
                solved[f, level] = value[f]
            values.append(value)
        return tuple(values)

    none = (zero,) * tracer_count
    top_values, bottom_values = lax.fori_loop(0, half, inward, (none, none), unroll=2)
    across = 1.0 / (1.0 - top * bottom)
    up, down = [], []
    for f in range(tracer_count):
        upper_value = (top_values[f] - top * bottom_values[f]) * across
        lower_value = bottom_values[f] - bottom * upper_value
        solved[f, half - 1] = upper_value
        solved[f, half] = lower_value
        up.append(upper_value)
        down.append(lower_value)

    def outward(step, carry):
        values = []
        for level, before in ((half - 2 - step, carry[0]), (half + 1 + step, carry[1])):
            value = tuple(
                solved[f, level] - factor[level] * before[f] for f in range(tracer_count)
            )
            for f in range(tracer_count):
                solved[f, level] = value[f]
            values.append(value)
        return tuple(values)

    lax.fori_loop(0, half - 1, outward, (tuple(up), tuple(down)), unroll=2)
    store = pltpu.make_async_copy(solved, new_hbm, local_sem.at[6])
    store.start()

    for copy in search_copies:
        copy.wait_recv()

    def operator(v):
        return (
            diagonal * v
            - east_weight * next_col(v)
            - west_weight * last_col(v)
            - north_weight * next_row(v)
            - south_weight * last_row(v)
        )

    wide_image = operator(search[...])
    wide_second = inverse * wide_image
    image = centre(wide_image)
    second = centre(wide_second)
    second_image = centre(operator(wide_second))

    for k, field in enumerate((forcing, image, second, second_image)):
        fields[k] = field

    def rows_sum(v):
        return jnp.sum(v, axis=0, keepdims=True)

    products = (
        rows_sum(forcing * first),
        rows_sum(first * image),
        rows_sum(image * second),
        rows_sum(second * second_image),
    )
    tile_row = lax.broadcasted_iota(jnp.int32, (8, cols), 0)
    sums = jnp.zeros((8, cols), jnp.float32)
    for k, product in enumerate(products):
        sums = jnp.where(tile_row == k, product, sums)
    sums = jnp.sum(sums, axis=1, keepdims=True)
    place = lax.broadcasted_iota(jnp.int32, (1, cols), 1)
    line = jnp.zeros((1, cols), jnp.float32)
    for k in range(4):
        line = jnp.where(place == k, sums[k : k + 1], line)
    reduce_copies = []
    slot_copies = []
    for stage in range(3):
        partial[stage] = line
        copies = [
            remote(
                REDUCE + stage * (GROUP - 1) + k - 1,
                partial.at[stage],
                gathered.at[stage, k - 1],
                partner(stage, k),
            )
            for k in range(1, GROUP)
        ]
        reduce_copies += copies
        if stage == 0:
            slot_copies = [
                remote(SLOT, fields, fields_near.at[0], beside(0, 1)),
                remote(SLOT + 1, fields, fields_near.at[1], beside(0, -1)),
            ]
        for k, copy in enumerate(copies):
            copy.wait_recv()
            line = line + gathered[stage, k]
    rho, bend, gap, tail = (
        jnp.sum(jnp.where(place == k, line, 0.0), axis=1, keepdims=True) for k in range(4)
    )
    step0 = rho / bend
    rho_next = rho - 2.0 * step0 * bend + step0 * step0 * gap
    ratio = rho_next / rho
    cross = bend - step0 * gap
    inner = bend - 2.0 * step0 * gap + step0 * step0 * tail
    step1 = rho_next / (inner + 2.0 * ratio * cross + ratio * ratio * bend)
    along_first = step0 + step1 * (1.0 + ratio)
    along_second = -step1 * step0

    for copy in slot_copies:
        copy.wait_recv()
    for k, ref in enumerate((fields_near.at[0], fields, fields_near.at[1])):
        nearby = search[8 : 8 + rows, k * cols : (k + 1) * cols]
        placed[0, k * rows : (k + 1) * rows, :] = along_first * nearby + along_second * ref[2]
        placed[1, k * rows : (k + 1) * rows, :] = (
            ref[0] - along_first * ref[1] - along_second * ref[3]
        )
    blocks = rows // block_rows
    slots = slots_ref.shape[1]
    for slot in range(slots):
        held = map_ref[0, gx * slots + slot]
        filled = jnp.where(held >= 0, 1.0, 0.0)
        safe = jnp.maximum(held, 0)
        offset = lax.rem(safe // blocks - gx + 1 + n_gx, n_gx)
        target = jnp.minimum(offset * blocks + lax.rem(safe, blocks), 3 * blocks - 1)
        begin = pl.ds(target * block_rows, block_rows)
        slots_ref[0, slot] = filled * placed[0, begin, :]
        slots_ref[1, slot] = filled * placed[1, begin, :]

    for copy in (
        meta_copies
        + atm_copies
        + near_copies[0]
        + near_copies[1]
        + edge_copies
        + search_copies + slot_copies + reduce_copies
    ):
        copy.wait_send()
    store.wait()


def on_device(
    atm_flux,
    remap_source,
    remap_weight,
    tracers,
    velocity,
    vert_diff,
    ocean_depth,
    surface_term,
    land_mask,
    barotropic_block_map,
):
    n_gy, n_gx = lax.axis_size("gy"), lax.axis_size("gx")
    tracer_count, levels, rows, cols = tracers.shape
    blocks = land_mask.shape[0]
    slots = barotropic_block_map.shape[1] // n_gx
    atm_blocks = atm_flux.shape[1]
    f32 = jnp.float32
    vmem = functools.partial(pltpu.VMEM, dtype=f32)
    in_vmem = pl.BlockSpec(memory_space=pltpu.VMEM)
    in_smem = pl.BlockSpec(memory_space=pltpu.SMEM)
    in_hbm = pl.BlockSpec(memory_space=pltpu.HBM)
    slot_shape = jax.ShapeDtypeStruct((2, slots, rows // blocks, cols), f32)
    new_tracers, in_slots = pl.pallas_call(
        functools.partial(kernel, n_gy, n_gx),
        out_shape=(jax.ShapeDtypeStruct(tracers.shape, f32), slot_shape),
        in_specs=[in_smem] * 3 + [in_hbm] * 7,
        out_specs=(in_hbm, in_vmem),
        scratch_shapes=[
            pltpu.VMEM(remap_weight.shape, remap_weight.dtype),
            vmem((tracer_count, levels, rows + 16, cols)),
            vmem((levels, rows, cols)),
            vmem((levels, rows + 8, cols)),
            vmem((levels + 1, rows, cols)),
            vmem((3, rows, cols)),
            vmem((3, rows + 16, 3 * cols)),
            pltpu.VMEM(atm_flux.shape, atm_flux.dtype),
            vmem((atm_blocks, tracer_count, cols)),
            vmem((3 * atm_blocks, tracer_count, cols)),
            vmem((levels, tracer_count, 2, cols)),
            vmem((levels, tracer_count, 2, cols)),
            vmem((levels, tracer_count, 2, cols)),
            vmem((levels, tracer_count, 2, cols)),
            vmem((64, cols)),
            vmem((64, cols)),
            vmem((2, tracer_count, rows, cols)),
            vmem((2, 2, tracer_count, rows, cols)),
            vmem((2, rows, cols)),
            vmem((2, rows, cols)),
            vmem((2, tracer_count, rows, cols)),
            vmem((2, tracer_count, rows, cols)),
            vmem((tracer_count, rows, cols)),
            vmem((levels, rows, cols)),
            vmem((levels, rows, cols)),
            vmem((levels, rows, cols)),
            vmem(tracers.shape),
            vmem((rows, cols)),
            vmem((rows + 16, 3 * cols)),
            vmem((4, rows, cols)),
            vmem((2, 4, rows, cols)),
            vmem((3, 1, cols)),
            vmem((3, GROUP - 1, 1, cols)),
            vmem((2, 3 * rows, cols)),
            pltpu.SemaphoreType.DMA((10,)),
            pltpu.SemaphoreType.DMA((COPIES,)),
            pltpu.SemaphoreType.DMA((COPIES,)),
        ],
        compiler_params=pltpu.CompilerParams(
            collective_id=0, has_side_effects=True, vmem_limit_bytes=VMEM_LIMIT
        ),
        name="ocean_window",
    )(
        jnp.transpose(remap_source, (1, 2, 0)),
        land_mask.T,
        barotropic_block_map,
        atm_flux,
        ocean_depth,
        surface_term,
        remap_weight,
        tracers,
        velocity,
        vert_diff,
    )
    return new_tracers, in_slots[:1], in_slots[1:]


def solution(mesh):
    return jax.shard_map(
        on_device,
        mesh=mesh,
        in_specs=(
            P("gy", "gx", None, None),
            P("gy", "gx", None),
            P("gy", "gx", None, None, None),
            P(None, None, "gy", "gx"),
            P(None, None, "gy", "gx"),
            P(None, "gy", "gx"),
            P("gy", "gx"),
            P("gy", "gx"),
            P("gy", "gx"),
            P("gy", None),
        ),
        out_specs=(P(None, None, "gy", "gx"), P("gy", "gx", None, None), P("gy", "gx", None, None)),
        check_vma=False,
    )
```

```python
import functools
import math

import jax
import jax.numpy as jnp
from jax import lax
from jax.experimental import pallas as pl
from jax.experimental.pallas import tpu as pltpu
from jax.sharding import PartitionSpec as P

DIFFUSIVITY = 0.1
FLUX_GAIN = 0.5
MESH = pl.DeviceIdType.MESH
GROUP = 8
VMEM_LIMIT = 67043328
SIDES = ((0, 1), (0, -1), (1, 0), (-1, 0), (1, 1), (1, -1), (-1, 1), (-1, -1))
META, ATM, EDGE, SEARCH, SLOT, REDUCE = 0, 8, 10, 18, 26, 28
COPIES = REDUCE + 3 * (GROUP - 1)


def flux(speed, behind, centre, forward, beyond, mixing):
    drop = centre - forward
    return (
        speed * (7.0 * (centre + forward) - (behind + beyond))
        - jnp.abs(speed) * (3.0 * drop + (beyond - behind))
        + mixing * drop
    )


def kernel(
    n_gy,
    n_gx,
    source_ref,
    land_ref,
    map_ref,
    atm_hbm,
    depth_hbm,
    surface_hbm,
    weight_hbm,
    tracer_hbm,
    velocity_hbm,
    vert_hbm,
    new_hbm,
    slots_ref,
    weight,
    cells,
    east_speed,
    north_speed,
    vert,
    meta_own,
    meta,
    atm_raw,
    atm_own,
    atm_near,
    to_north,
    to_south,
    from_south,
    from_north,
    speed_north,
    speed_south,
    edge_own,
    edge_near,
    speed_east,
    speed_west,
    west_face,
    beyond,
    surface_flux,
    factor,
    scale,
    gain,
    solved,
    search_own,
    search,
    fields,
    fields_near,
    partial,
    gathered,
    placed,
    local_sem,
    send_sem,
    recv_sem,
):
    tracer_count, levels, rows, cols = tracer_hbm.shape
    gy = lax.axis_index("gy")
    gx = lax.axis_index("gx")

    half = levels // 2
    loads = [
        pltpu.make_async_copy(
            tracer_hbm.at[:, part * half : (part + 1) * half],
            cells.at[:, part * half : (part + 1) * half, 8 : 8 + rows, :],
            local_sem.at[part],
        )
        for part in range(2)
    ]
    loads += [
        pltpu.make_async_copy(velocity_hbm.at[0], east_speed, local_sem.at[2]),
        pltpu.make_async_copy(
            velocity_hbm.at[1], north_speed.at[:, 8 : 8 + rows, :], local_sem.at[3]
        ),
        pltpu.make_async_copy(vert_hbm, vert.at[1:levels], local_sem.at[4]),
        pltpu.make_async_copy(weight_hbm, weight, local_sem.at[5]),
    ]
    small = [
        pltpu.make_async_copy(depth_hbm, meta_own.at[1], local_sem.at[7]),
        pltpu.make_async_copy(surface_hbm, meta_own.at[2], local_sem.at[8]),
        pltpu.make_async_copy(atm_hbm, atm_raw, local_sem.at[9]),
    ]
    for load in small + loads:
        load.start()

    def beside(dy, dx):
        return (lax.rem(gy + dy + n_gy, n_gy), lax.rem(gx + dx + n_gx, n_gx))

    inner_gy, inner_gx = n_gy // GROUP, n_gx // GROUP
    core, column = lax.rem(gy, inner_gy), lax.rem(gx, inner_gx)
    flat = core * inner_gx + column

    def partner(stage, k):
        if stage == 0:
            other = lax.rem(flat + k, GROUP)
            return (gy - core + other // inner_gx, gx - column + lax.rem(other, inner_gx))
        if stage == 1:
            return (gy, lax.rem(gx + k * inner_gx, n_gx))
        return (lax.rem(gy + k * inner_gy, n_gy), gx)

    barrier = pltpu.get_barrier_semaphore()
    peers = [beside(dy, dx) for dy, dx in SIDES]
    peers += [partner(stage, k) for stage in range(3) for k in range(1, GROUP)]
    for peer in peers:
        pl.semaphore_signal(barrier, inc=1, device_id=peer, device_id_type=MESH)

    def remote(index, src, dst, device):
        copy = pltpu.make_async_remote_copy(
            src_ref=src,
            dst_ref=dst,
            send_sem=send_sem.at[index],
            recv_sem=recv_sem.at[index],
            device_id=device,
            device_id_type=MESH,
        )
        copy.start()
        return copy

    def sides(first, own, padded):
        lead = (slice(None),) * (len(own.shape) - 2)
        source_rows = {0: slice(0, rows), 1: slice(rows - 8, rows), -1: slice(0, 8)}
        target_rows = {0: slice(8, 8 + rows), 1: slice(0, 8), -1: slice(8 + rows, 16 + rows)}
        target_cols = {
            0: slice(cols, 2 * cols),
            1: slice(0, cols),
            -1: slice(2 * cols, 3 * cols),
        }
        return [
            remote(
                first + k,
                own.at[lead + (source_rows[dy],)],
                padded.at[lead + (target_rows[dy], target_cols[dx])],
                beside(dy, dx),
            )
            for k, (dy, dx) in enumerate(SIDES)
        ]

    row = lax.broadcasted_iota(jnp.int32, (rows, cols), 0)
    lane = lax.broadcasted_iota(jnp.int32, (rows, cols), 1)
    block_rows = rows // land_ref.shape[1]
    mask = jnp.zeros((rows, cols), jnp.float32)
    for block in range(land_ref.shape[1]):
        wet = land_ref[0, block].astype(jnp.float32)
        mask = jnp.where(row // block_rows == block, wet, mask)
    meta_own[0] = mask
    for load in small:
        load.wait()
    for k in range(3):
        meta[k, 8 : 8 + rows, cols : 2 * cols] = meta_own[k]
    atm_own[...] = atm_raw[0].astype(jnp.float32)
    blocks_near = atm_own.shape[0]
    atm_near[blocks_near : 2 * blocks_near] = atm_own[...]

    zero = jnp.zeros((rows, cols), jnp.float32)
    group = lane // 4

    def pack(part, level, packed):
        index = level - part * half
        kept = []
        for f in range(tracer_count):
            values = cells[f, level, 8 : 8 + rows, :] * mask
            cells[f, level, 8 : 8 + rows, :] = values
            to_north[level, f] = values[rows - 2 :]
            to_south[level, f] = values[:2]
            turned = pltpu.roll(values, 4 * index + 2, 1)
            kept.append(jnp.where(group == index, turned, packed[f]))
        return tuple(kept)

    def row_copies(part):
        span = slice(part * half, (part + 1) * half)
        return [
            remote(EDGE + 2 * part, to_north.at[span], from_south.at[span], beside(1, 0)),
            remote(EDGE + 2 * part + 1, to_south.at[span], from_north.at[span], beside(-1, 0)),
        ]

    loads[0].wait()
    packed = lax.fori_loop(
        0, half, functools.partial(pack, 0), (zero,) * tracer_count, unroll=4
    )
    for f in range(tracer_count):
        edge_own[0, f] = packed[f]
    pl.semaphore_wait(barrier, len(peers))
    near_copies = [row_copies(0)]
    meta_copies = sides(META, meta_own, meta)
    atm_copies = [
        remote(ATM, atm_own, atm_near.at[0:blocks_near], beside(0, 1)),
        remote(ATM + 1, atm_own, atm_near.at[2 * blocks_near : 3 * blocks_near], beside(0, -1)),
    ]
    loads[1].wait()
    packed = lax.fori_loop(
        half, levels, functools.partial(pack, 1), (zero,) * tracer_count, unroll=4
    )
    near_copies.append(row_copies(1))
    for f in range(tracer_count):
        edge_own[1, f] = packed[f]
    edge_copies = [
        remote(EDGE + 4, edge_own, edge_near.at[0], beside(0, -1)),
        remote(EDGE + 5, edge_own, edge_near.at[1], beside(0, 1)),
    ]

    loads[2].wait()
    loads[3].wait()

    def pack_speed(part, level, packed):
        index = level - part * half
        speed_north[pl.ds(level, 1), :] = north_speed[level, 7 + rows : 8 + rows, :]
        turned = pltpu.roll(east_speed[level], 4 * index + 1, 1)
        return jnp.where(group == index, turned, packed)

    for part in range(2):
        speed_east[part] = lax.fori_loop(
            part * half, (part + 1) * half, functools.partial(pack_speed, part), zero, unroll=4
        )
    edge_copies += [
        remote(EDGE + 6, speed_north, speed_south, beside(1, 0)),
        remote(EDGE + 7, speed_east, speed_west, beside(0, 1)),
    ]

    loads[4].wait()
    vert[0] = zero
    vert[levels] = zero

    def eliminate(step, carry):
        top, bottom = carry
        low, high = step, levels - 1 - step
        lower, upper = vert[low], vert[low + 1]
        share = 1.0 / (1.0 + lower + upper + lower * top)
        top = -upper * share
        factor[low] = top
        scale[low] = share
        gain[low] = lower * share
        lower, upper = vert[high], vert[high + 1]
        share = 1.0 / (1.0 + lower + upper + upper * bottom)
        bottom = -lower * share
        factor[high] = bottom
        scale[high] = share
        gain[high] = upper * share
        return top, bottom

    top, bottom = lax.fori_loop(0, half, eliminate, (zero, zero))

    loads[5].wait()
    for copy in atm_copies:
        copy.wait_recv()

    def remap(r, carry):
        total = jnp.zeros((tracer_count, cols), jnp.float32)
        for k in range(weight.shape[2]):
            picked = atm_near[source_ref[0, k, r]].astype(jnp.bfloat16)
            total += lax.dot_general(
                picked,
                weight[r, 0, k],
                (((1,), (1,)), ((), ())),
                preferred_element_type=jnp.float32,
            )
        for f in range(tracer_count):
            surface_flux[f, pl.ds(r, 1), :] = total[f : f + 1]
        return carry

    lax.fori_loop(0, rows, remap, 0, unroll=4)
    for f in range(tracer_count):
        surface_flux[f] = FLUX_GAIN * mask * surface_flux[f]

    for copy in meta_copies:
        copy.wait_recv()
    height, width = search.shape
    wide_row = lax.broadcasted_iota(jnp.int32, (height, width), 0)
    below = jnp.where(gy > 0, 1.0, 0.0)
    above = jnp.where(gy < n_gy - 1, 1.0, 0.0)
    inside = jnp.where(wide_row < 8, below, jnp.where(wide_row >= 8 + rows, above, 1.0))
    wide_mask = meta[0] * inside
    depth = meta[1]

    def next_col(v):
        return pltpu.roll(v, width - 1, 1)

    def last_col(v):
        return pltpu.roll(v, 1, 1)

    def next_row(v):
        return pltpu.roll(v, height - 1, 0)

    def last_row(v):
        return pltpu.roll(v, 1, 0)

    wide_east = wide_mask * next_col(wide_mask)
    wide_north = wide_mask * next_row(wide_mask)
    east_weight = wide_east * (depth + next_col(depth)) * 0.5
    north_weight = wide_north * (depth + next_row(depth)) * 0.5
    west_weight = last_col(east_weight)
    south_weight = last_row(north_weight)
    diagonal = (
        wide_mask * meta[2]
        + (1.0 - wide_mask)
        + east_weight
        + west_weight
        + north_weight
        + south_weight
    )
    inverse = 1.0 / diagonal
    wide_south = last_row(wide_north)
    wide_west = last_col(wide_east)

    def centre(v):
        return v[8 : 8 + rows, cols : 2 * cols]

    east_open = centre(wide_east) * (1.0 / 12.0)
    north_open = centre(wide_north) * (1.0 / 12.0)
    south_open = centre(wide_south) * (1.0 / 12.0)
    west_open = jnp.broadcast_to(centre(wide_west)[:, :1], (rows, cols)) * (1.0 / 12.0)
    mask_south = wide_mask[6:8, cols : 2 * cols]
    mask_north = wide_mask[8 + rows : 10 + rows, cols : 2 * cols]

    for copy in edge_copies:
        copy.wait_recv()

    for part in range(2):
        for f in range(tracer_count):
            behind = edge_near[1, part, f]
            ahead = edge_own[part, f]
            west_face[part, f] = flux(
                speed_west[part] * west_open,
                behind,
                pltpu.roll(behind, cols - 1, 1),
                pltpu.roll(ahead, cols - 2, 1),
                pltpu.roll(ahead, cols - 3, 1),
                (12.0 * DIFFUSIVITY) * west_open,
            )
            beyond[part, f] = jnp.where(lane % 4 < 2, behind, edge_near[0, part, f])

    def coefficients(speed, mixing):
        size = jnp.abs(speed)
        common, tilt = 7.0 * speed, 3.0 * size - mixing
        return size - speed, common - tilt, common + tilt, size + speed

    def advected(part, level):
        back_e, centre_e, next_e, far_e = coefficients(east_speed[level] * east_open, mix_east)
        back_n, centre_n, next_n, far_n = coefficients(
            north_speed[level, 8 : 8 + rows, :] * north_open, mix_north
        )
        back_s, centre_s, next_s, far_s = coefficients(
            north_speed[level, 7 : 7 + rows, :] * south_open, mix_south
        )
        at_here = centre_n - next_s
        at_north = next_n + far_s
        at_south = back_n - centre_s
        turn = 4 * (level - part * half)
        results = []
        for f in range(tracer_count):
            here = cells[f, level, 8 : 8 + rows, :]
            south1 = cells[f, level, 7 : 7 + rows, :]
            south2 = cells[f, level, 6 : 6 + rows, :]
            north1 = cells[f, level, 9 : 9 + rows, :]
            north2 = cells[f, level, 10 : 10 + rows, :]
            outer = pltpu.roll(beyond[part, f], lax.rem(2 * cols - 2 - turn, cols), 1)
            east2 = pltpu.roll(jnp.where(lane < 2, outer, here), cols - 2, 1)
            east1 = pltpu.roll(jnp.where(lane < 1, outer, here), cols - 1, 1)
            west1 = pltpu.roll(jnp.where(lane == cols - 1, outer, here), 1, 1)
            east_flux = (centre_e * here + next_e * east1) + (back_e * west1 - far_e * east2)
            west_flux = jnp.where(
                lane == 0,
                pltpu.roll(west_face[part, f], lax.rem(cols - turn, cols), 1),
                pltpu.roll(east_flux, 1, 1),
            )
            spread = (at_here * here + at_north * north1) + (
                at_south * south1 - (far_n * north2 + back_s * south2)
            )
            results.append(mask * (here - (east_flux - west_flux) - spread))
        return results

    mix_east = (12.0 * DIFFUSIVITY) * east_open
    mix_north = (12.0 * DIFFUSIVITY) * north_open
    mix_south = (12.0 * DIFFUSIVITY) * south_open

    def put(level, carry):
        for f in range(tracer_count):
            cells[f, level, 6:8, :] = from_south[level, f] * mask_south
            cells[f, level, 8 + rows : 10 + rows, :] = from_north[level, f] * mask_north
        north_speed[level, 7:8, :] = speed_south[pl.ds(level, 1), :]
        return carry

    def advect(part, level, total):
        provisional = advected(part, level)
        for f in range(tracer_count):
            solved[f, level] = provisional[f]
        return total + (provisional[0] - provisional[1])

    total = surface_flux[0] - surface_flux[1]
    for part in range(2):
        for copy in near_copies[part]:
            copy.wait_recv()
        lax.fori_loop(part * half, (part + 1) * half, put, 0, unroll=4)
        total = lax.fori_loop(
            part * half, (part + 1) * half, functools.partial(advect, part), total, unroll=2
        )
    for f in range(tracer_count):
        solved[f, 0] = solved[f, 0] + surface_flux[f]

    forcing = mask * total * (1.0 / math.sqrt(2.0 * levels))
    first = centre(inverse) * forcing
    search_own[...] = first
    search[8 : 8 + rows, cols : 2 * cols] = first
    search_copies = sides(SEARCH, search_own, search)

    def inward(step, carry):
        low, high = step, levels - 1 - step
        values = []
        for level, before in ((low, carry[0]), (high, carry[1])):
            value = tuple(
                solved[f, level] * scale[level] + gain[level] * before[f]
                for f in range(tracer_count)
            )
            for f in range(tracer_count):
                solved[f, level] = value[f]
            values.append(value)
        return tuple(values)

    none = (zero,) * tracer_count
    top_values, bottom_values = lax.fori_loop(0, half, inward, (none, none), unroll=2)
    across = 1.0 / (1.0 - top * bottom)
    up, down = [], []
    for f in range(tracer_count):
        upper_value = (top_values[f] - top * bottom_values[f]) * across
        lower_value = bottom_values[f] - bottom * upper_value
        solved[f, half - 1] = upper_value
        solved[f, half] = lower_value
        up.append(upper_value)
        down.append(lower_value)

    def outward(step, carry):
        values = []
        for level, before in ((half - 2 - step, carry[0]), (half + 1 + step, carry[1])):
            value = tuple(
                solved[f, level] - factor[level] * before[f] for f in range(tracer_count)
            )
            for f in range(tracer_count):
                solved[f, level] = value[f]
            values.append(value)
        return tuple(values)

    lax.fori_loop(0, half - 1, outward, (tuple(up), tuple(down)), unroll=2)
    store = pltpu.make_async_copy(solved, new_hbm, local_sem.at[6])
    store.start()

    for copy in search_copies:
        copy.wait_recv()

    def operator(v):
        return (
            diagonal * v
            - east_weight * next_col(v)
            - west_weight * last_col(v)
            - north_weight * next_row(v)
            - south_weight * last_row(v)
        )

    wide_image = operator(search[...])
    wide_second = inverse * wide_image
    image = centre(wide_image)
    second = centre(wide_second)
    second_image = centre(operator(wide_second))

    for k, field in enumerate((forcing, image, second, second_image)):
        fields[k] = field

    def rows_sum(v):
        return jnp.sum(v, axis=0, keepdims=True)

    products = (
        rows_sum(forcing * first),
        rows_sum(first * image),
        rows_sum(image * second),
        rows_sum(second * second_image),
    )
    tile_row = lax.broadcasted_iota(jnp.int32, (8, cols), 0)
    sums = jnp.zeros((8, cols), jnp.float32)
    for k, product in enumerate(products):
        sums = jnp.where(tile_row == k, product, sums)
    sums = jnp.sum(sums, axis=1, keepdims=True)
    place = lax.broadcasted_iota(jnp.int32, (1, cols), 1)
    line = jnp.zeros((1, cols), jnp.float32)
    for k in range(4):
        line = jnp.where(place == k, sums[k : k + 1], line)
    reduce_copies = []
    slot_copies = []
    for stage in range(3):
        partial[stage] = line
        copies = [
            remote(
                REDUCE + stage * (GROUP - 1) + k - 1,
                partial.at[stage],
                gathered.at[stage, k - 1],
                partner(stage, k),
            )
            for k in range(1, GROUP)
        ]
        reduce_copies += copies
        if stage == 0:
            slot_copies = [
                remote(SLOT, fields, fields_near.at[0], beside(0, 1)),
                remote(SLOT + 1, fields, fields_near.at[1], beside(0, -1)),
            ]
        for k, copy in enumerate(copies):
            copy.wait_recv()
            line = line + gathered[stage, k]
    rho, bend, gap, tail = (
        jnp.sum(jnp.where(place == k, line, 0.0), axis=1, keepdims=True) for k in range(4)
    )
    step0 = rho / bend
    rho_next = rho - 2.0 * step0 * bend + step0 * step0 * gap
    ratio = rho_next / rho
    cross = bend - step0 * gap
    inner = bend - 2.0 * step0 * gap + step0 * step0 * tail
    step1 = rho_next / (inner + 2.0 * ratio * cross + ratio * ratio * bend)
    along_first = step0 + step1 * (1.0 + ratio)
    along_second = -step1 * step0

    for copy in slot_copies:
        copy.wait_recv()
    for k, ref in enumerate((fields_near.at[0], fields, fields_near.at[1])):
        nearby = search[8 : 8 + rows, k * cols : (k + 1) * cols]
        placed[0, k * rows : (k + 1) * rows, :] = along_first * nearby + along_second * ref[2]
        placed[1, k * rows : (k + 1) * rows, :] = (
            ref[0] - along_first * ref[1] - along_second * ref[3]
        )
    blocks = rows // block_rows
    slots = slots_ref.shape[1]
    for slot in range(slots):
        held = map_ref[0, gx * slots + slot]
        filled = jnp.where(held >= 0, 1.0, 0.0)
        safe = jnp.maximum(held, 0)
        offset = lax.rem(safe // blocks - gx + 1 + n_gx, n_gx)
        target = jnp.minimum(offset * blocks + lax.rem(safe, blocks), 3 * blocks - 1)
        begin = pl.ds(target * block_rows, block_rows)
        slots_ref[0, slot] = filled * placed[0, begin, :]
        slots_ref[1, slot] = filled * placed[1, begin, :]

    for copy in (
        meta_copies
        + atm_copies
        + near_copies[0]
        + near_copies[1]
        + edge_copies
        + search_copies + slot_copies + reduce_copies
    ):
        copy.wait_send()
    store.wait()


def on_device(
    atm_flux,
    remap_source,
    remap_weight,
    tracers,
    velocity,
    vert_diff,
    ocean_depth,
    surface_term,
    land_mask,
    barotropic_block_map,
):
    n_gy, n_gx = lax.axis_size("gy"), lax.axis_size("gx")
    tracer_count, levels, rows, cols = tracers.shape
    blocks = land_mask.shape[0]
    slots = barotropic_block_map.shape[1] // n_gx
    atm_blocks = atm_flux.shape[1]
    f32 = jnp.float32
    vmem = functools.partial(pltpu.VMEM, dtype=f32)
    in_vmem = pl.BlockSpec(memory_space=pltpu.VMEM)
    in_smem = pl.BlockSpec(memory_space=pltpu.SMEM)
    in_hbm = pl.BlockSpec(memory_space=pltpu.HBM)
    slot_shape = jax.ShapeDtypeStruct((2, slots, rows // blocks, cols), f32)
    new_tracers, in_slots = pl.pallas_call(
        functools.partial(kernel, n_gy, n_gx),
        out_shape=(jax.ShapeDtypeStruct(tracers.shape, f32), slot_shape),
        in_specs=[in_smem] * 3 + [in_hbm] * 7,
        out_specs=(in_hbm, in_vmem),
        scratch_shapes=[
            pltpu.VMEM(remap_weight.shape, remap_weight.dtype),
            vmem((tracer_count, levels, rows + 16, cols)),
            vmem((levels, rows, cols)),
            vmem((levels, rows + 8, cols)),
            vmem((levels + 1, rows, cols)),
            vmem((3, rows, cols)),
            vmem((3, rows + 16, 3 * cols)),
            pltpu.VMEM(atm_flux.shape, atm_flux.dtype),
            vmem((atm_blocks, tracer_count, cols)),
            vmem((3 * atm_blocks, tracer_count, cols)),
            vmem((levels, tracer_count, 2, cols)),
            vmem((levels, tracer_count, 2, cols)),
            vmem((levels, tracer_count, 2, cols)),
            vmem((levels, tracer_count, 2, cols)),
            vmem((64, cols)),
            vmem((64, cols)),
            vmem((2, tracer_count, rows, cols)),
            vmem((2, 2, tracer_count, rows, cols)),
            vmem((2, rows, cols)),
            vmem((2, rows, cols)),
            vmem((2, tracer_count, rows, cols)),
            vmem((2, tracer_count, rows, cols)),
            vmem((tracer_count, rows, cols)),
            vmem((levels, rows, cols)),
            vmem((levels, rows, cols)),
            vmem((levels, rows, cols)),
            vmem(tracers.shape),
            vmem((rows, cols)),
            vmem((rows + 16, 3 * cols)),
            vmem((4, rows, cols)),
            vmem((2, 4, rows, cols)),
            vmem((3, 1, cols)),
            vmem((3, GROUP - 1, 1, cols)),
            vmem((2, 3 * rows, cols)),
            pltpu.SemaphoreType.DMA((10,)),
            pltpu.SemaphoreType.DMA((COPIES,)),
            pltpu.SemaphoreType.DMA((COPIES,)),
        ],
        compiler_params=pltpu.CompilerParams(
            collective_id=0, has_side_effects=True, vmem_limit_bytes=VMEM_LIMIT
        ),
        name="ocean_window",
    )(
        jnp.transpose(remap_source, (1, 2, 0)),
        land_mask.T,
        barotropic_block_map,
        atm_flux,
        ocean_depth,
        surface_term,
        remap_weight,
        tracers,
        velocity,
        vert_diff,
    )
    return new_tracers, in_slots[:1], in_slots[1:]


def solution(mesh):
    return jax.shard_map(
        on_device,
        mesh=mesh,
        in_specs=(
            P("gy", "gx", None, None),
            P("gy", "gx", None),
            P("gy", "gx", None, None, None),
            P(None, None, "gy", "gx"),
            P(None, None, "gy", "gx"),
            P(None, "gy", "gx"),
            P("gy", "gx"),
            P("gy", "gx"),
            P("gy", "gx"),
            P("gy", None),
        ),
        out_specs=(P(None, None, "gy", "gx"), P("gy", "gx", None, None), P("gy", "gx", None, None)),
        check_vma=False,
    )
```

```python
import functools
import math

import jax
import jax.numpy as jnp
from jax import lax
from jax.experimental import pallas as pl
from jax.experimental.pallas import tpu as pltpu
from jax.sharding import PartitionSpec as P

DIFFUSIVITY = 0.1
FLUX_GAIN = 0.5
MESH = pl.DeviceIdType.MESH
GROUP = 8
VMEM_LIMIT = 67043328
SIDES = ((0, 1), (0, -1), (1, 0), (-1, 0), (1, 1), (1, -1), (-1, 1), (-1, -1))
META, ATM, EDGE, SEARCH, SLOT, REDUCE = 0, 8, 10, 18, 26, 28
COPIES = REDUCE + 3 * (GROUP - 1)


def kernel(
    n_gy,
    n_gx,
    source_ref,
    land_ref,
    map_ref,
    atm_hbm,
    depth_hbm,
    surface_hbm,
    weight_hbm,
    tracer_hbm,
    velocity_hbm,
    vert_hbm,
    new_hbm,
    slots_ref,
    weight,
    cells,
    east_speed,
    north_speed,
    vert,
    meta_own,
    meta,
    atm_raw,
    atm_own,
    atm_near,
    to_north,
    to_south,
    from_south,
    from_north,
    speed_north,
    speed_south,
    edge_own,
    edge_near,
    speed_east,
    speed_west,
    beyond,
    surface_flux,
    factor,
    scale,
    gain,
    solved,
    search_own,
    search,
    fields,
    fields_near,
    partial,
    gathered,
    placed,
    local_sem,
    send_sem,
    recv_sem,
):
    tracer_count, levels, rows, cols = tracer_hbm.shape
    gy = lax.axis_index("gy")
    gx = lax.axis_index("gx")

    half = levels // 2
    loads = [
        pltpu.make_async_copy(
            tracer_hbm.at[:, part * half : (part + 1) * half],
            cells.at[:, part * half : (part + 1) * half, 8 : 8 + rows, :],
            local_sem.at[part],
        )
        for part in range(2)
    ]
    loads += [
        pltpu.make_async_copy(velocity_hbm.at[0], east_speed, local_sem.at[2]),
        pltpu.make_async_copy(
            velocity_hbm.at[1], north_speed.at[:, 8 : 8 + rows, :], local_sem.at[3]
        ),
        pltpu.make_async_copy(vert_hbm, vert.at[1:levels], local_sem.at[4]),
        pltpu.make_async_copy(weight_hbm, weight, local_sem.at[5]),
    ]
    small = [
        pltpu.make_async_copy(depth_hbm, meta_own.at[1], local_sem.at[7]),
        pltpu.make_async_copy(surface_hbm, meta_own.at[2], local_sem.at[8]),
        pltpu.make_async_copy(atm_hbm, atm_raw, local_sem.at[9]),
    ]
    for load in small + loads:
        load.start()

    def beside(dy, dx):
        return (lax.rem(gy + dy + n_gy, n_gy), lax.rem(gx + dx + n_gx, n_gx))

    inner_gy, inner_gx = n_gy // GROUP, n_gx // GROUP
    core, column = lax.rem(gy, inner_gy), lax.rem(gx, inner_gx)
    flat = core * inner_gx + column

    def partner(stage, k):
        if stage == 0:
            other = lax.rem(flat + k, GROUP)
            return (gy - core + other // inner_gx, gx - column + lax.rem(other, inner_gx))
        if stage == 1:
            return (gy, lax.rem(gx + k * inner_gx, n_gx))
        return (lax.rem(gy + k * inner_gy, n_gy), gx)

    barrier = pltpu.get_barrier_semaphore()
    peers = [beside(dy, dx) for dy, dx in SIDES]
    peers += [partner(stage, k) for stage in range(3) for k in range(1, GROUP)]
    for peer in peers:
        pl.semaphore_signal(barrier, inc=1, device_id=peer, device_id_type=MESH)

    def remote(index, src, dst, device):
        copy = pltpu.make_async_remote_copy(
            src_ref=src,
            dst_ref=dst,
            send_sem=send_sem.at[index],
            recv_sem=recv_sem.at[index],
            device_id=device,
            device_id_type=MESH,
        )
        copy.start()
        return copy

    def sides(first, own, padded):
        lead = (slice(None),) * (len(own.shape) - 2)
        source_rows = {0: slice(0, rows), 1: slice(rows - 8, rows), -1: slice(0, 8)}
        target_rows = {0: slice(8, 8 + rows), 1: slice(0, 8), -1: slice(8 + rows, 16 + rows)}
        target_cols = {
            0: slice(cols, 2 * cols),
            1: slice(0, cols),
            -1: slice(2 * cols, 3 * cols),
        }
        return [
            remote(
                first + k,
                own.at[lead + (source_rows[dy],)],
                padded.at[lead + (target_rows[dy], target_cols[dx])],
                beside(dy, dx),
            )
            for k, (dy, dx) in enumerate(SIDES)
        ]

    row = lax.broadcasted_iota(jnp.int32, (rows, cols), 0)
    lane = lax.broadcasted_iota(jnp.int32, (rows, cols), 1)
    block_rows = rows // land_ref.shape[1]
    mask = jnp.zeros((rows, cols), jnp.float32)
    for block in range(land_ref.shape[1]):
        wet = land_ref[0, block].astype(jnp.float32)
        mask = jnp.where(row // block_rows == block, wet, mask)
    meta_own[0] = mask
    for load in small:
        load.wait()
    for k in range(3):
        meta[k, 8 : 8 + rows, cols : 2 * cols] = meta_own[k]
    atm_own[...] = atm_raw[0].astype(jnp.float32)
    blocks_near = atm_own.shape[0]
    atm_near[blocks_near : 2 * blocks_near] = atm_own[...]

    zero = jnp.zeros((rows, cols), jnp.float32)
    group = lane // 4

    def pack(part, level, packed):
        index = level - part * half
        kept = []
        for f in range(tracer_count):
            values = cells[f, level, 8 : 8 + rows, :] * mask
            cells[f, level, 8 : 8 + rows, :] = values
            to_north[level, f] = values[rows - 2 :]
            to_south[level, f] = values[:2]
            turned = pltpu.roll(values, 4 * index + 2, 1)
            kept.append(jnp.where(group == index, turned, packed[f]))
        return tuple(kept)

    def row_copies(part):
        span = slice(part * half, (part + 1) * half)
        return [
            remote(EDGE + 2 * part, to_north.at[span], from_south.at[span], beside(1, 0)),
            remote(EDGE + 2 * part + 1, to_south.at[span], from_north.at[span], beside(-1, 0)),
        ]

    loads[0].wait()
    packed = lax.fori_loop(
        0, half, functools.partial(pack, 0), (zero,) * tracer_count, unroll=4
    )
    for f in range(tracer_count):
        edge_own[0, f] = packed[f]
    pl.semaphore_wait(barrier, len(peers))
    near_copies = [row_copies(0)]
    meta_copies = sides(META, meta_own, meta)
    atm_copies = [
        remote(ATM, atm_own, atm_near.at[0:blocks_near], beside(0, 1)),
        remote(ATM + 1, atm_own, atm_near.at[2 * blocks_near : 3 * blocks_near], beside(0, -1)),
    ]
    loads[1].wait()
    packed = lax.fori_loop(
        half, levels, functools.partial(pack, 1), (zero,) * tracer_count, unroll=4
    )
    near_copies.append(row_copies(1))
    for f in range(tracer_count):
        edge_own[1, f] = packed[f]
    edge_copies = [
        remote(EDGE + 4, edge_own, edge_near.at[0], beside(0, -1)),
        remote(EDGE + 5, edge_own, edge_near.at[1], beside(0, 1)),
    ]

    loads[2].wait()
    loads[3].wait()

    def pack_speed(part, level, packed):
        index = level - part * half
        speed_north[pl.ds(level, 1), :] = north_speed[level, 7 + rows : 8 + rows, :]
        turned = pltpu.roll(east_speed[level], 4 * index + 1, 1)
        return jnp.where(group == index, turned, packed)

    for part in range(2):
        speed_east[part] = lax.fori_loop(
            part * half, (part + 1) * half, functools.partial(pack_speed, part), zero, unroll=4
        )
    edge_copies += [
        remote(EDGE + 6, speed_north, speed_south, beside(1, 0)),
        remote(EDGE + 7, speed_east, speed_west, beside(0, 1)),
    ]

    loads[4].wait()
    vert[0] = zero
    vert[levels] = zero

    def eliminate(step, carry):
        top, bottom = carry
        low, high = step, levels - 1 - step
        lower, upper = vert[low], vert[low + 1]
        share = 1.0 / (1.0 + lower + upper + lower * top)
        top = -upper * share
        factor[low] = top
        scale[low] = share
        gain[low] = lower * share
        lower, upper = vert[high], vert[high + 1]
        share = 1.0 / (1.0 + lower + upper + upper * bottom)
        bottom = -lower * share
        factor[high] = bottom
        scale[high] = share
        gain[high] = upper * share
        return top, bottom

    top, bottom = lax.fori_loop(0, half, eliminate, (zero, zero))

    loads[5].wait()
    for copy in atm_copies:
        copy.wait_recv()

    def remap(r, carry):
        total = jnp.zeros((tracer_count, cols), jnp.float32)
        for k in range(weight.shape[2]):
            picked = atm_near[source_ref[0, k, r]].astype(jnp.bfloat16)
            total += lax.dot_general(
                picked,
                weight[r, 0, k],
                (((1,), (1,)), ((), ())),
                preferred_element_type=jnp.float32,
            )
        for f in range(tracer_count):
            surface_flux[f, pl.ds(r, 1), :] = total[f : f + 1]
        return carry

    lax.fori_loop(0, rows, remap, 0, unroll=4)
    for f in range(tracer_count):
        surface_flux[f] = FLUX_GAIN * mask * surface_flux[f]

    for copy in meta_copies:
        copy.wait_recv()
    height, width = search.shape
    wide_row = lax.broadcasted_iota(jnp.int32, (height, width), 0)
    below = jnp.where(gy > 0, 1.0, 0.0)
    above = jnp.where(gy < n_gy - 1, 1.0, 0.0)
    inside = jnp.where(wide_row < 8, below, jnp.where(wide_row >= 8 + rows, above, 1.0))
    wide_mask = meta[0] * inside
    depth = meta[1]

    def next_col(v):
        return pltpu.roll(v, width - 1, 1)

    def last_col(v):
        return pltpu.roll(v, 1, 1)

    def next_row(v):
        return pltpu.roll(v, height - 1, 0)

    def last_row(v):
        return pltpu.roll(v, 1, 0)

    wide_east = wide_mask * next_col(wide_mask)
    wide_north = wide_mask * next_row(wide_mask)
    east_weight = wide_east * (depth + next_col(depth)) * 0.5
    north_weight = wide_north * (depth + next_row(depth)) * 0.5
    west_weight = last_col(east_weight)
    south_weight = last_row(north_weight)
    diagonal = (
        wide_mask * meta[2]
        + (1.0 - wide_mask)
        + east_weight
        + west_weight
        + north_weight
        + south_weight
    )
    inverse = 1.0 / diagonal
    wide_south = last_row(wide_north)
    wide_west = last_col(wide_east)

    def centre(v):
        return v[8 : 8 + rows, cols : 2 * cols]

    east_open = centre(wide_east) * (1.0 / 12.0)
    north_open = centre(wide_north) * (1.0 / 12.0)
    south_open = centre(wide_south) * (1.0 / 12.0)
    west_open = centre(wide_west) * (1.0 / 12.0)
    mask_south = wide_mask[6:8, cols : 2 * cols]
    mask_north = wide_mask[8 + rows : 10 + rows, cols : 2 * cols]

    for copy in edge_copies:
        copy.wait_recv()

    for part in range(2):
        for f in range(tracer_count):
            behind = edge_near[1, part, f]
            beyond[part, f] = jnp.where(lane % 4 < 2, behind, edge_near[0, part, f])

    def coefficients(speed, mixing):
        size = jnp.abs(speed)
        common, tilt = 7.0 * speed, 3.0 * size - mixing
        return size - speed, common - tilt, common + tilt, size + speed

    def advected(part, level):
        back_e, centre_e, next_e, far_e = coefficients(east_speed[level] * east_open, mix_east)
        back_n, centre_n, next_n, far_n = coefficients(
            north_speed[level, 8 : 8 + rows, :] * north_open, mix_north
        )
        back_s, centre_s, next_s, far_s = coefficients(
            north_speed[level, 7 : 7 + rows, :] * south_open, mix_south
        )
        turn = 4 * (level - part * half)
        arriving = pltpu.roll(speed_west[part], cols - 1 - turn, 1)
        speed = pltpu.roll(jnp.where(lane == cols - 1, arriving, east_speed[level]), 1, 1)
        back_w, centre_w, next_w, far_w = coefficients(speed * west_open, mix_west)
        at_here = (centre_n - next_s) + (centre_e - next_w)
        at_east = next_e + far_w
        at_west = back_e - centre_w
        at_north = next_n + far_s
        at_south = back_n - centre_s
        results = []
        for f in range(tracer_count):
            here = cells[f, level, 8 : 8 + rows, :]
            south1 = cells[f, level, 7 : 7 + rows, :]
            south2 = cells[f, level, 6 : 6 + rows, :]
            north1 = cells[f, level, 9 : 9 + rows, :]
            north2 = cells[f, level, 10 : 10 + rows, :]
            outer = pltpu.roll(beyond[part, f], lax.rem(2 * cols - 2 - turn, cols), 1)
            east2 = pltpu.roll(jnp.where(lane < 2, outer, here), cols - 2, 1)
            east1 = pltpu.roll(jnp.where(lane < 1, outer, here), cols - 1, 1)
            west1 = pltpu.roll(jnp.where(lane == cols - 1, outer, here), 1, 1)
            west2 = pltpu.roll(jnp.where(lane >= cols - 2, outer, here), 2, 1)
            along = (at_east * east1 - far_e * east2) + (at_west * west1 - back_w * west2)
            spread = (at_here * here + at_north * north1) + (
                at_south * south1 - (far_n * north2 + back_s * south2)
            )
            results.append(mask * (here - along - spread))
        return results

    mix_east = (12.0 * DIFFUSIVITY) * east_open
    mix_west = (12.0 * DIFFUSIVITY) * west_open
    mix_north = (12.0 * DIFFUSIVITY) * north_open
    mix_south = (12.0 * DIFFUSIVITY) * south_open

    def put(level, carry):
        for f in range(tracer_count):
            cells[f, level, 6:8, :] = from_south[level, f] * mask_south
            cells[f, level, 8 + rows : 10 + rows, :] = from_north[level, f] * mask_north
        north_speed[level, 7:8, :] = speed_south[pl.ds(level, 1), :]
        return carry

    def advect(part, level, total):
        provisional = advected(part, level)
        for f in range(tracer_count):
            solved[f, level] = provisional[f]
        return total + (provisional[0] - provisional[1])

    total = surface_flux[0] - surface_flux[1]
    for part in range(2):
        for copy in near_copies[part]:
            copy.wait_recv()
        lax.fori_loop(part * half, (part + 1) * half, put, 0, unroll=4)
        total = lax.fori_loop(
            part * half, (part + 1) * half, functools.partial(advect, part), total, unroll=2
        )
    for f in range(tracer_count):
        solved[f, 0] = solved[f, 0] + surface_flux[f]

    forcing = mask * total * (1.0 / math.sqrt(2.0 * levels))
    first = centre(inverse) * forcing
    search_own[...] = first
    search[8 : 8 + rows, cols : 2 * cols] = first
    search_copies = sides(SEARCH, search_own, search)

    def inward(step, carry):
        low, high = step, levels - 1 - step
        values = []
        for level, before in ((low, carry[0]), (high, carry[1])):
            value = tuple(
                solved[f, level] * scale[level] + gain[level] * before[f]
                for f in range(tracer_count)
            )
            for f in range(tracer_count):
                solved[f, level] = value[f]
            values.append(value)
        return tuple(values)

    none = (zero,) * tracer_count
    top_values, bottom_values = lax.fori_loop(0, half, inward, (none, none), unroll=2)
    across = 1.0 / (1.0 - top * bottom)
    up, down = [], []
    for f in range(tracer_count):
        upper_value = (top_values[f] - top * bottom_values[f]) * across
        lower_value = bottom_values[f] - bottom * upper_value
        solved[f, half - 1] = upper_value
        solved[f, half] = lower_value
        up.append(upper_value)
        down.append(lower_value)

    def outward(step, carry):
        values = []
        for level, before in ((half - 2 - step, carry[0]), (half + 1 + step, carry[1])):
            value = tuple(
                solved[f, level] - factor[level] * before[f] for f in range(tracer_count)
            )
            for f in range(tracer_count):
                solved[f, level] = value[f]
            values.append(value)
        return tuple(values)

    lax.fori_loop(0, half - 1, outward, (tuple(up), tuple(down)), unroll=2)
    store = pltpu.make_async_copy(solved, new_hbm, local_sem.at[6])
    store.start()

    for copy in search_copies:
        copy.wait_recv()

    def operator(v):
        return (
            diagonal * v
            - east_weight * next_col(v)
            - west_weight * last_col(v)
            - north_weight * next_row(v)
            - south_weight * last_row(v)
        )

    wide_image = operator(search[...])
    wide_second = inverse * wide_image
    image = centre(wide_image)
    second = centre(wide_second)
    second_image = centre(operator(wide_second))

    for k, field in enumerate((forcing, image, second, second_image)):
        fields[k] = field

    def rows_sum(v):
        return jnp.sum(v, axis=0, keepdims=True)

    products = (
        rows_sum(forcing * first),
        rows_sum(first * image),
        rows_sum(image * second),
        rows_sum(second * second_image),
    )
    tile_row = lax.broadcasted_iota(jnp.int32, (8, cols), 0)
    sums = jnp.zeros((8, cols), jnp.float32)
    for k, product in enumerate(products):
        sums = jnp.where(tile_row == k, product, sums)
    sums = jnp.sum(sums, axis=1, keepdims=True)
    place = lax.broadcasted_iota(jnp.int32, (1, cols), 1)
    line = jnp.zeros((1, cols), jnp.float32)
    for k in range(4):
        line = jnp.where(place == k, sums[k : k + 1], line)
    reduce_copies = []
    slot_copies = []
    for stage in range(3):
        partial[stage] = line
        copies = [
            remote(
                REDUCE + stage * (GROUP - 1) + k - 1,
                partial.at[stage],
                gathered.at[stage, k - 1],
                partner(stage, k),
            )
            for k in range(1, GROUP)
        ]
        reduce_copies += copies
        if stage == 0:
            slot_copies = [
                remote(SLOT, fields, fields_near.at[0], beside(0, 1)),
                remote(SLOT + 1, fields, fields_near.at[1], beside(0, -1)),
            ]
        for k, copy in enumerate(copies):
            copy.wait_recv()
            line = line + gathered[stage, k]
    rho, bend, gap, tail = (
        jnp.sum(jnp.where(place == k, line, 0.0), axis=1, keepdims=True) for k in range(4)
    )
    step0 = rho / bend
    rho_next = rho - 2.0 * step0 * bend + step0 * step0 * gap
    ratio = rho_next / rho
    cross = bend - step0 * gap
    inner = bend - 2.0 * step0 * gap + step0 * step0 * tail
    step1 = rho_next / (inner + 2.0 * ratio * cross + ratio * ratio * bend)
    along_first = step0 + step1 * (1.0 + ratio)
    along_second = -step1 * step0

    for copy in slot_copies:
        copy.wait_recv()
    for k, ref in enumerate((fields_near.at[0], fields, fields_near.at[1])):
        nearby = search[8 : 8 + rows, k * cols : (k + 1) * cols]
        placed[0, k * rows : (k + 1) * rows, :] = along_first * nearby + along_second * ref[2]
        placed[1, k * rows : (k + 1) * rows, :] = (
            ref[0] - along_first * ref[1] - along_second * ref[3]
        )
    blocks = rows // block_rows
    slots = slots_ref.shape[1]
    for slot in range(slots):
        held = map_ref[0, gx * slots + slot]
        filled = jnp.where(held >= 0, 1.0, 0.0)
        safe = jnp.maximum(held, 0)
        offset = lax.rem(safe // blocks - gx + 1 + n_gx, n_gx)
        target = jnp.minimum(offset * blocks + lax.rem(safe, blocks), 3 * blocks - 1)
        begin = pl.ds(target * block_rows, block_rows)
        slots_ref[0, slot] = filled * placed[0, begin, :]
        slots_ref[1, slot] = filled * placed[1, begin, :]

    for copy in (
        meta_copies
        + atm_copies
        + near_copies[0]
        + near_copies[1]
        + edge_copies
        + search_copies + slot_copies + reduce_copies
    ):
        copy.wait_send()
    store.wait()


def on_device(
    atm_flux,
    remap_source,
    remap_weight,
    tracers,
    velocity,
    vert_diff,
    ocean_depth,
    surface_term,
    land_mask,
    barotropic_block_map,
):
    n_gy, n_gx = lax.axis_size("gy"), lax.axis_size("gx")
    tracer_count, levels, rows, cols = tracers.shape
    blocks = land_mask.shape[0]
    slots = barotropic_block_map.shape[1] // n_gx
    atm_blocks = atm_flux.shape[1]
    f32 = jnp.float32
    vmem = functools.partial(pltpu.VMEM, dtype=f32)
    in_vmem = pl.BlockSpec(memory_space=pltpu.VMEM)
    in_smem = pl.BlockSpec(memory_space=pltpu.SMEM)
    in_hbm = pl.BlockSpec(memory_space=pltpu.HBM)
    slot_shape = jax.ShapeDtypeStruct((2, slots, rows // blocks, cols), f32)
    new_tracers, in_slots = pl.pallas_call(
        functools.partial(kernel, n_gy, n_gx),
        out_shape=(jax.ShapeDtypeStruct(tracers.shape, f32), slot_shape),
        in_specs=[in_smem] * 3 + [in_hbm] * 7,
        out_specs=(in_hbm, in_vmem),
        scratch_shapes=[
            pltpu.VMEM(remap_weight.shape, remap_weight.dtype),
            vmem((tracer_count, levels, rows + 16, cols)),
            vmem((levels, rows, cols)),
            vmem((levels, rows + 8, cols)),
            vmem((levels + 1, rows, cols)),
            vmem((3, rows, cols)),
            vmem((3, rows + 16, 3 * cols)),
            pltpu.VMEM(atm_flux.shape, atm_flux.dtype),
            vmem((atm_blocks, tracer_count, cols)),
            vmem((3 * atm_blocks, tracer_count, cols)),
            vmem((levels, tracer_count, 2, cols)),
            vmem((levels, tracer_count, 2, cols)),
            vmem((levels, tracer_count, 2, cols)),
            vmem((levels, tracer_count, 2, cols)),
            vmem((64, cols)),
            vmem((64, cols)),
            vmem((2, tracer_count, rows, cols)),
            vmem((2, 2, tracer_count, rows, cols)),
            vmem((2, rows, cols)),
            vmem((2, rows, cols)),
            vmem((2, tracer_count, rows, cols)),
            vmem((tracer_count, rows, cols)),
            vmem((levels, rows, cols)),
            vmem((levels, rows, cols)),
            vmem((levels, rows, cols)),
            vmem(tracers.shape),
            vmem((rows, cols)),
            vmem((rows + 16, 3 * cols)),
            vmem((4, rows, cols)),
            vmem((2, 4, rows, cols)),
            vmem((3, 1, cols)),
            vmem((3, GROUP - 1, 1, cols)),
            vmem((2, 3 * rows, cols)),
            pltpu.SemaphoreType.DMA((10,)),
            pltpu.SemaphoreType.DMA((COPIES,)),
            pltpu.SemaphoreType.DMA((COPIES,)),
        ],
        compiler_params=pltpu.CompilerParams(
            collective_id=0, has_side_effects=True, vmem_limit_bytes=VMEM_LIMIT
        ),
        name="ocean_window",
    )(
        jnp.transpose(remap_source, (1, 2, 0)),
        land_mask.T,
        barotropic_block_map,
        atm_flux,
        ocean_depth,
        surface_term,
        remap_weight,
        tracers,
        velocity,
        vert_diff,
    )
    return new_tracers, in_slots[:1], in_slots[1:]


def solution(mesh):
    return jax.shard_map(
        on_device,
        mesh=mesh,
        in_specs=(
            P("gy", "gx", None, None),
            P("gy", "gx", None),
            P("gy", "gx", None, None, None),
            P(None, None, "gy", "gx"),
            P(None, None, "gy", "gx"),
            P(None, "gy", "gx"),
            P("gy", "gx"),
            P("gy", "gx"),
            P("gy", "gx"),
            P("gy", None),
        ),
        out_specs=(P(None, None, "gy", "gx"), P("gy", "gx", None, None), P("gy", "gx", None, None)),
        check_vma=False,
    )
```
